32 devices in a mesh: comp: 8 (over y, x, core), tile: 4 (over z).
Axes of the slice: x: 2, y: 2, z: 4, core: 2. Of those that a mesh axis runs over, the one named last changes fastest.
Arguments:
- spectrum: bfloat16 [1296, 128, 1024], P('comp', 'tile'), may hold values from 0.049804688 to 1
- courant_x: float32 [1296], replicated, may hold values from -0.45 to 0.45
- courant_y: float32 [1296], replicated, may hold values from -0.45 to 0.45
- growth: float32 [1296], replicated, may hold values from 0.02 to 0.2
- dissipation: float32 [1296], replicated, may hold values from 0.1 to 1
- bin_width: float32 [1296], replicated, may hold values from 0.00038580247 to 0.0030864198
- transfer: bfloat16 [1296, 1296], replicated, may hold values from -0.15625 to 0.15625
- stress_weights: float32 [2, 1296], replicated, may hold values from -0.15625 to 0.15625
- orbital_weights: float32 [1296], replicated, may hold values from 0.000154321 to 0.0015432099
- wind: float32 [128, 1024], P('tile', 'comp'), may hold values from 1 to 10
- wave_wet: int32 [128, 1024], P('tile', 'comp'), may hold values 0 or 1
- owner: int32 [4, 8, 32, 128, 1], P('tile', 'comp'), may hold values from 0 to 31; in each aligned block of 4096 rows (0 to 4095, 4096 to 8191, ..., all dimensions but the last counted through in order) at most 384 rows name the same one
- cell_index: int32 [4, 8, 32, 128], P('tile', 'comp'), may hold values from 0 to 2047
- current_stress: float32 [2, 64, 1024], P(None, 'tile', 'comp'), may hold values from -3 to 3
- sediment: float32 [4, 64, 1024], P(None, 'tile', 'comp'), may hold values from 0.1 to 2
- metals: float32 [4, 64, 1024], P(None, 'tile', 'comp'), may hold values from 0.1 to 2
- bed_class: int32 [64, 1024], P('tile', 'comp'), may hold values from 0 to 3
- roms_wet: int32 [64, 1024], P('tile', 'comp'), may hold values 0 or 1
- class_props: float32 [3, 4], replicated, may hold values from 0.2 to 0.8
- partition: float32 [4, 4], replicated, may hold values from 0.3 to 3
Outputs:
- spectrum_new: bfloat16 [1296, 128, 1024], P(None, 'tile', 'comp')
- sediment_new: float32 [4, 64, 1024], P(None, 'tile', 'comp')
- dissolved: float32 [4, 64, 1024], P(None, 'tile', 'comp')
- sorbed: float32 [4, 64, 1024], P(None, 'tile', 'comp')
The draws below stay inside these ranges and needn't reach their ends.
Inputs may be any that keep to these rules, and one draw needn't show every extreme that they name: `owner`: within each aligned block of 4096 points (one device's points, in order), no tile is named more than 384 times, a bound that some block reaches.
All inputs are finite; a program needn't handle non-finite values. No bound on the sum of `wave_wet` or of `roms_wet` on one device may be relied on, other than what follows from the above.
Results may differ from the reference program's by a relative error of at most 0.0049.
Values may be sent and summed in bfloat16 or wider, within the bound.
A program may use at most 192 MiB of HBM per device.

```python
import math
import jax
import jax.numpy as jnp
import numpy as np
from jax import lax

NSED = 4
NMET = 4
ROWS_DEV = 32
COLS_DEV = 128
RR = 16
RC = 128
K = 1296
GX = 128
GY = 1024
RX = 64
RY = 1024
CELLS = 2048
CAP = 384
N_COMP = 8
N_TILE = 4
DEVICES = 32


def place_ends(drawn, rng, least, top_value):
    extent = drawn.shape
    spot = [jax.random.randint(jax.random.fold_in(rng, axis), (), 0, extent[axis]) for axis in range(len(extent))]
    drawn = drawn.at[tuple(spot)].set(least)
    longest = extent.index(max(extent))
    spot[longest] = (spot[longest] + 1) % extent[longest]
    return drawn.at[tuple(spot)].set(top_value)


def levels(rng, extent, cuts, smallest, high):
    factor_of = 1.0
    for position, blocks in cuts:
        steps = jax.random.uniform(jax.random.fold_in(jax.random.fold_in(rng, 6), position), (blocks,), jnp.float32, smallest / len(cuts), high / len(cuts))
        factor_of = factor_of * jnp.repeat(jnp.exp(steps), extent[position] // blocks).reshape((-1,) + (1,) * (len(extent) - 1 - position))
    return factor_of


def routed_block(key, own, number, rows, number_of, top, bound, slope):
    sequence = jax.random.permutation(key, number_of)
    heavy_load, common = load_shares(number_of, rows * top, bound, slope, True), load_shares(number_of, rows * top, bound, slope, False)
    places = jnp.arange(number_of)

    def named(tallies, turn):
        used = int((tallies > 0).sum())
        fixed = max(1, used // 4)
        shifted = fixed + (places - fixed + turn * (used - fixed)) % max(1, number_of - fixed)
        return jnp.zeros((number_of,), jnp.int32).at[sequence[jnp.where(places < fixed, places, shifted)]].set(jnp.asarray(tallies, jnp.int32))

    tallies = jnp.where(number % 4 == 0, named(heavy_load, number // 4), named(common, number - number // 4 - 1))
    mixed = jax.random.permutation(jax.random.fold_in(own, 3), number_of)
    donor, taker = mixed[0:number_of // 2 * 2:2], mixed[1:number_of // 2 * 2:2]
    room = jnp.minimum(tallies[donor] - 1, bound - tallies[taker]) // 2
    room = jnp.where((donor == sequence[0]) | (taker == sequence[0]) | (tallies[taker] == 0), 0, jnp.maximum(room, 0))
    shifted = jax.random.randint(jax.random.fold_in(own, 4), (number_of // 2,), 0, 1 << 20) % (room + 1)
    tallies = tallies.at[donor].add(-shifted).at[taker].add(shifted)
    items = jnp.searchsorted(jnp.cumsum(tallies), jnp.arange(rows * top), side="right").astype(jnp.int32)
    table = items.reshape(top, rows).T
    table = table[jax.random.permutation(jax.random.fold_in(own, 1), rows)]
    turn = jax.random.randint(jax.random.fold_in(own, 2), (rows, 1), 0, top)
    return jnp.take_along_axis(table, (jnp.arange(top)[None, :] + turn) % top, axis=1)


def load_shares(amount, total, most, slope, full):
    weights = [(1 << 20) // math.isqrt(rank ** slope) + 1 for rank in range(1, amount + 1)]
    largest = most if full else min(most, max(-(-total // amount), total * weights[0] // sum(weights)))
    least = 1 if total - largest >= amount - 1 else 0
    given, rest = [largest] + [least] * (amount - 1), total - largest - least * (amount - 1)
    while rest > 0:
        candidates = [i for i in range(1, amount) if given[i] < largest] or [i for i in range(1, amount) if given[i] < most]
        whole, remaining = sum([weights[i] for i in candidates]), rest
        for i in candidates:
            extra = min(most - given[i], max(1, remaining * weights[i] // whole), rest)
            given[i] = given[i] + extra
            rest = rest - extra
    return np.array(given)


def scatter_about(key, extent, deviation, bound, shards=(), held_as=jnp.bfloat16):
    level = levels(key, extent, shards, -0.22, 0.18) if shards else 1.0
    entries = jax.random.normal(key, extent, jnp.float32) * deviation * level
    return jnp.minimum(jnp.maximum(entries, -bound), bound).astype(held_as)


def setup_inputs(seed: int = 0) -> dict:
    key_of = jax.random.split(jax.random.key(seed), 21)
    spectrum = jnp.clip(0.049804688 + 0.9501953 * jax.random.uniform(key_of[0], (K, GX, GY), jnp.float32) ** levels(key_of[0], (K, GX, GY), ((0, 8), (1, 4)), -0.2, 0.2), 0.049804688, 1.0).astype(jnp.bfloat16)
    courant_x = jnp.clip(jax.random.uniform(key_of[1], (K,), jnp.float32, -0.45, 0.45), -0.45, 0.45)
    courant_y = jnp.clip(jax.random.uniform(key_of[2], (K,), jnp.float32, -0.45, 0.45), -0.45, 0.45)
    growth = jnp.clip(jnp.exp(jax.random.uniform(key_of[3], (K,), jnp.float32, math.log(0.02), math.log(0.2))), 0.02, 0.2)
    dissipation = jnp.clip(jnp.exp(jax.random.uniform(key_of[4], (K,), jnp.float32, math.log(0.1), math.log(1.0))), 0.1, 1.0)
    bin_width = jnp.clip(jnp.exp(jax.random.uniform(key_of[5], (K,), jnp.float32, math.log(0.00038580247), math.log(0.0030864198))), 0.00038580247, 0.0030864198)
    transfer = scatter_about(key_of[6], (K, K), K ** -0.5, 0.15625)
    stress_weights = scatter_about(key_of[7], (2, K), K ** -0.5, 0.15625, (), jnp.float32)
    orbital_weights = jnp.clip(jnp.exp(jax.random.uniform(key_of[8], (K,), jnp.float32, math.log(0.000154321), math.log(0.0015432099))), 0.000154321, 0.0015432099)
    wind = jnp.clip(jnp.exp(math.log(10.0) - 2.3025851 * jax.random.uniform(key_of[9], (GX, GY), jnp.float32) ** levels(key_of[9], (GX, GY), ((0, 4), (1, 8)), -0.2, 0.2)), 1.0, 10.0)
    wave_wet = place_ends((jax.random.randint(key_of[10], (GX, GY), 0, 5) < 4).astype(jnp.int32), jax.random.fold_in(key_of[10], 1), 0, 1)
    owner_keys = jax.random.split(jax.random.fold_in(key_of[11], 1), N_TILE * N_COMP * ROWS_DEV * COLS_DEV // (ROWS_DEV * COLS_DEV))
    owner_turns = jax.random.permutation(jax.random.fold_in(key_of[11], 3), N_TILE * N_COMP * ROWS_DEV * COLS_DEV // (ROWS_DEV * COLS_DEV))
    owner = jax.vmap(lambda own, number: routed_block(jax.random.fold_in(key_of[11], 2), own, number, ROWS_DEV * COLS_DEV, DEVICES, 1, CAP, 2))(owner_keys, owner_turns).reshape((N_TILE, N_COMP, ROWS_DEV, COLS_DEV, 1))
    cell_index = place_ends(jax.random.randint(key_of[12], (N_TILE, N_COMP, ROWS_DEV, COLS_DEV), 0, CELLS), jax.random.fold_in(key_of[12], 1), 0, CELLS - 1).astype(jnp.int32)
    current_stress = scatter_about(key_of[13], (2, RX, RY), 0.5, 3.0, ((1, 4), (2, 8)), jnp.float32)
    sediment = jnp.clip(jnp.exp(math.log(2.0) - 2.9957323 * jax.random.uniform(key_of[14], (NSED, RX, RY), jnp.float32) ** levels(key_of[14], (NSED, RX, RY), ((1, 4), (2, 8)), -0.2, 0.2)), 0.1, 2.0)
    metals = jnp.clip(jnp.exp(math.log(2.0) - 2.9957323 * jax.random.uniform(key_of[15], (NMET, RX, RY), jnp.float32) ** levels(key_of[15], (NMET, RX, RY), ((1, 4), (2, 8)), -0.2, 0.2)), 0.1, 2.0)
    bed_class = place_ends(jax.random.randint(key_of[16], (RX, RY), 0, NSED), jax.random.fold_in(key_of[16], 1), 0, NSED - 1).astype(jnp.int32)
    roms_wet = place_ends((jax.random.randint(key_of[17], (RX, RY), 0, 8) < 7).astype(jnp.int32), jax.random.fold_in(key_of[17], 1), 0, 1)
    class_props = jnp.clip(jnp.exp(jax.random.uniform(key_of[18], (3, NSED), jnp.float32, math.log(0.2), math.log(0.8))), 0.2, 0.8)
    partition = jnp.clip(jnp.exp(jax.random.uniform(key_of[19], (NMET, NSED), jnp.float32, math.log(0.3), math.log(3.0))), 0.3, 3.0)
    return {"spectrum": spectrum, "courant_x": courant_x, "courant_y": courant_y, "growth": growth, "dissipation": dissipation, "bin_width": bin_width, "transfer": transfer, "stress_weights": stress_weights, "orbital_weights": orbital_weights, "wind": wind, "wave_wet": wave_wet, "owner": owner, "cell_index": cell_index, "current_stress": current_stress, "sediment": sediment, "metals": metals, "bed_class": bed_class, "roms_wet": roms_wet, "class_props": class_props, "partition": partition}


WAVE_STEP = 0.5
SEDIMENT_STEP = 1.0
DIFFUSION = 0.2

def upwind(padded, speed_x, speed_y):
    centre = padded[..., 1:-1, 1:-1]
    north = padded[..., :-2, 1:-1]
    south = padded[..., 2:, 1:-1]
    west = padded[..., 1:-1, :-2]
    east = padded[..., 1:-1, 2:]
    return centre - jnp.maximum(speed_x, 0.0) * (centre - north) - jnp.minimum(speed_x, 0.0) * (south - centre) - jnp.maximum(speed_y, 0.0) * (centre - west) - jnp.minimum(speed_y, 0.0) * (east - centre)

def diffuse(fields, wetness):
    padded = jnp.pad(fields, ((0, 0), (1, 1), (1, 1)))
    centre = padded[:, 1:-1, 1:-1]
    beside_all = padded[:, :-2, 1:-1] + padded[:, 2:, 1:-1] + padded[:, 1:-1, :-2] + padded[:, 1:-1, 2:]
    return wetness * (centre + DIFFUSION * (beside_all - 4.0 * centre))

def reference(spectrum, courant_x, courant_y, growth, dissipation, bin_width, transfer, stress_weights, orbital_weights, wind, wave_wet, owner, cell_index, current_stress, sediment, metals, bed_class, roms_wet, class_props, partition):

    def propagate_one(items):
        field, speed_x, speed_y = items
        padded = jnp.pad(field.astype(jnp.float32), 1)
        return upwind(padded, speed_x, speed_y).astype(jnp.bfloat16)
    propagated = lax.map(propagate_one, (spectrum, courant_x, courant_y))
    weights_all = jnp.concatenate([stress_weights, orbital_weights[None, :]], axis=0)

    def source_row(items):
        index, wind_row, wet_row = items
        row = lax.dynamic_index_in_dim(propagated, index, 1, keepdims=False)
        mixed = jnp.dot(transfer, row, preferred_element_type=jnp.float32)
        energy_row = row.astype(jnp.float32)
        total = jnp.dot(bin_width, energy_row, precision=lax.Precision.HIGHEST)
        ratio = total / (total + 1.0)
        part = energy_row + WAVE_STEP * (mixed - dissipation[:, None] * ratio[None, :] * energy_row)
        relaxed = part + WAVE_STEP * growth[:, None] * wind_row[None, :] * energy_row
        fresh = wet_row.astype(jnp.float32)[None, :] * jnp.maximum(relaxed, 0.0)
        forces = jnp.dot(weights_all, fresh, precision=lax.Precision.HIGHEST)
        return (fresh.astype(jnp.bfloat16), forces)
    rows_new, forces_rows = lax.map(source_row, (jnp.arange(GX, dtype=jnp.int32), wind, wave_wet))
    spectrum_new = jnp.transpose(rows_new, (1, 0, 2))
    forces = jnp.transpose(forces_rows, (1, 0, 2))
    forces = forces.reshape(3, N_TILE, ROWS_DEV, N_COMP, COLS_DEV).transpose(0, 1, 3, 2, 4)
    target = owner[..., 0]
    target_tile = target % N_TILE
    target_comp = target // N_TILE
    place = (target_tile * RR + cell_index // RC) * RY + target_comp * RC + cell_index % RC
    bottom = jnp.zeros((3, RX * RY), jnp.float32).at[:, place.reshape(-1).astype(jnp.int32)].add(forces.reshape(3, -1))
    bottom = bottom.reshape(3, RX, RY)
    shear_x = current_stress[0] + bottom[0]
    shear_y = current_stress[1] + bottom[1]
    shear = jnp.sqrt(shear_x * shear_x + shear_y * shear_y + bottom[2])
    low_share = 0.5 / NSED
    high_share = 1.0 - (NSED - 1) * low_share
    classes = jnp.arange(NSED, dtype=jnp.int32)[:, None, None]
    fraction = jnp.where(bed_class[None, :, :] == classes, high_share, low_share)
    erosion = class_props[0][:, None, None] * fraction * jnp.maximum(shear[None] / class_props[1][:, None, None] - 1.0, 0.0)
    wetness = roms_wet.astype(jnp.float32)
    settled = wetness * (sediment + SEDIMENT_STEP * (erosion - class_props[2][:, None, None] * sediment))
    carried = wetness * metals
    diffused = diffuse(jnp.concatenate([settled, carried], axis=0), wetness)
    sediment_new = diffused[:NSED]
    spread = diffused[NSED:]
    denominator = 1.0 + jnp.einsum('ms,sxy->mxy', partition, sediment_new, precision=lax.Precision.HIGHEST)
    dissolved = spread / denominator
    sorbed = spread - dissolved
    return (spectrum_new, sediment_new, dissolved, sorbed)
```

```python
import functools

import jax
import jax.numpy as jnp
from jax import lax
from jax.experimental import pallas as pl
from jax.experimental.pallas import tpu as pltpu
from jax.sharding import PartitionSpec as P

WAVE_STEP = 0.5
SEDIMENT_STEP = 1.0
DIFFUSION = 0.2
LANES = 128
PACK = 16
PAIR = 2
QUARTER = 8
PARTS = 4
F32 = jnp.float32
BF16 = jnp.bfloat16


def nt_dot(a, b):
    return lax.dot_general(a, b, (((1,), (1,)), ((), ())), preferred_element_type=F32)


def split_two(values):
    high = values.astype(BF16)
    return high, (values - high.astype(F32)).astype(BF16)


def step_kernel(
    n,
    n_tile,
    slots,
    x_hbm,
    cx_hbm,
    cy_hbm,
    grow_hbm,
    damp_hbm,
    bin_hbm,
    transfer_hbm,
    stress_hbm,
    orbital_hbm,
    wind_hbm,
    wet_hbm,
    owner_hbm,
    cell_hbm,
    current_hbm,
    sediment_hbm,
    metals_hbm,
    bed_hbm,
    roms_hbm,
    props_hbm,
    out,
    result,
    cx,
    cy,
    growth,
    dissipation,
    bins,
    table,
    stress,
    orbital,
    wind,
    wet,
    owner,
    cell,
    current,
    sediment,
    metals,
    bed,
    roms,
    props,
    columns,
    coef,
    xs,
    send,
    recv,
    rest_f,
    rest_send,
    rest_recv,
    whole,
    acc,
    stage,
    weights,
    rank,
    base,
    packed_acc,
    packed,
    got,
    targets,
    lifted,
    fields,
    edge_s,
    edge_r,
    small_sem,
    in_sem,
    table_sem,
    z_send,
    z_recv,
    send_sem,
    recv_sem,
    rest_ssem,
    rest_rsem,
    route_ssem,
    route_rsem,
    halo_ssem,
    halo_rsem,
):
    me = lax.axis_index("comp")
    tile = lax.axis_index("tile")
    devices = n * n_tile
    number = me * n_tile + tile
    own, rows, width = x_hbm.shape
    cols = width // n
    full = n * own
    main = own // PACK * PACK
    rest = own - main
    groups = main // PACK + (1 if rest else 0)
    steps = rows // PAIR
    halves = rows // PACK
    nb = -(-slots // LANES)
    cells_r, cells_c = result.shape[1], result.shape[2]
    is_top, is_bottom = tile == 0, tile == n_tile - 1
    is_left, is_right = me == 0, me == n - 1
    mesh_id = pl.DeviceIdType.MESH
    above = {"tile": lax.rem(tile + n_tile - 1, n_tile)}
    below = {"tile": lax.rem(tile + 1, n_tile)}
    west_of = {"comp": lax.rem(me + n - 1, n)}
    east_of = {"comp": lax.rem(me + 1, n)}

    barrier = pltpu.get_barrier_semaphore()

    @pl.loop(1, devices)
    def _(o):
        t = lax.rem(number + o, devices)
        pl.semaphore_signal(
            barrier,
            inc=1,
            device_id={"comp": t // n_tile, "tile": lax.rem(t, n_tile)},
            device_id_type=mesh_id,
        )

    smalls = [
        (cx_hbm, cx),
        (cy_hbm, cy),
        (bin_hbm, bins),
        (stress_hbm, stress),
        (orbital_hbm, orbital),
        (grow_hbm, growth),
        (damp_hbm, dissipation),
        (wind_hbm, wind),
        (wet_hbm, wet),
        (owner_hbm, owner),
        (cell_hbm, cell),
        (current_hbm, current),
        (sediment_hbm, sediment),
        (metals_hbm, metals),
        (bed_hbm, bed),
        (roms_hbm, roms),
        (props_hbm, props),
    ]

    def small(i):
        return pltpu.make_async_copy(smalls[i][0], smalls[i][1], small_sem.at[i])

    def load(h, d):
        return pltpu.make_async_copy(
            x_hbm.at[:, pl.ds(h * PACK, PACK), pl.ds(d * cols, cols)],
            out.at[pl.ds(d * own, own), pl.ds(h * PACK, PACK), :],
            in_sem.at[h, d],
        )

    small(0).start()
    small(1).start()
    for h in range(halves):
        for d in range(n):
            load(h, d).start()
    for i in range(2, len(smalls)):
        small(i).start()
    get_table = pltpu.make_async_copy(transfer_hbm, table.at[pl.ds(0, full)], table_sem.at[0])
    get_table.start()

    def to_columns(values, i):
        for b in range(0, full, LANES):
            size = min(LANES, full - b)
            line = values[pl.ds(b, size)].reshape(1, size)
            columns[i, b : b + size, :] = jnp.broadcast_to(line, (LANES, size)).T

    small(0).wait()
    small(1).wait()
    to_columns(cx, 0)
    to_columns(cy, 1)

    for g in range(groups):
        first = g * PACK if g * PACK < main else own - PACK
        speed_x = columns[0, pl.ds(me * own + first, PACK), :]
        speed_y = columns[1, pl.ds(me * own + first, PACK), :]
        part = slice(g * PACK, (g + 1) * PACK)
        coef[0, part, :] = 1.0 - jnp.abs(speed_x) - jnp.abs(speed_y)
        coef[1, part, :] = jnp.maximum(speed_x, 0.0)
        coef[2, part, :] = -jnp.minimum(speed_x, 0.0)
        coef[3, part, :] = jnp.maximum(speed_y, 0.0)
        coef[4, part, :] = -jnp.minimum(speed_y, 0.0)

    @pl.when(is_top)
    def _():
        xs[0] = jnp.zeros(xs.shape[1:], BF16)
        edge_r[0] = jnp.zeros(edge_r.shape[1:], F32)

    @pl.when(is_bottom)
    def _():
        xs[rows + 1] = jnp.zeros(xs.shape[1:], BF16)
        edge_r[1] = jnp.zeros(edge_r.shape[1:], F32)

    @pl.when(is_left)
    def _():
        edge_r[2] = jnp.zeros(edge_r.shape[1:], F32)

    @pl.when(is_right)
    def _():
        edge_r[3] = jnp.zeros(edge_r.shape[1:], F32)

    def turn_in(c, is_first):
        top = c * QUARTER
        for d in range(n):
            if is_first:
                load(top // PACK, d).wait()

            def piece(at, first):
                block = out[pl.ds(d * own + first, PACK), top : top + QUARTER, :].astype(F32)
                xs[1 + top : 1 + top + QUARTER, pl.ds(at, PACK), d * cols : (d + 1) * cols] = (
                    jnp.swapaxes(block, 0, 1).astype(BF16)
                )

            @pl.loop(0, main // PACK)
            def _(g):
                start = pl.multiple_of(g * PACK, PACK)
                piece(start, start)

            if rest:
                piece(main, own - PACK)

    def upwind(row, start, is_rest):
        part = pl.ds(start, PACK)
        lane = lax.broadcasted_iota(jnp.int32, (PACK, cols), 1)
        first_lane, last_lane = lane == 0, lane == cols - 1
        kept, from_north, from_south, from_west, from_east = [coef[i, part, :] for i in range(5)]

        def tile_of(at, d):
            return xs[at, part, d * cols : (d + 1) * cols].astype(F32)

        centre = [tile_of(row + 1, d) for d in range(n)]
        right = [pltpu.roll(c, 1, 1) for c in centre]
        left = [pltpu.roll(c, cols - 1, 1) for c in centre]
        nothing = jnp.zeros((PACK, cols), F32)
        for d in range(n):
            west = jnp.where(first_lane, right[d - 1] if d else nothing, right[d])
            east = jnp.where(last_lane, left[d + 1] if d < n - 1 else nothing, left[d])
            moved = (
                kept * centre[d]
                + from_north * tile_of(row, d)
                + from_south * tile_of(row + 2, d)
                + from_west * west
                + from_east * east
            )
            if is_rest:
                rest_f[d, pl.ds(row * rest, rest), :] = moved[PACK - rest :]
            else:
                send[d, row, part, :] = moved.astype(BF16)

    def remote(q, o, source, target):
        return pltpu.make_async_remote_copy(
            src_ref=send.at[target, pl.ds(q * PAIR, PAIR)],
            dst_ref=recv.at[source, pl.ds(q * PAIR, PAIR)],
            send_sem=send_sem.at[o - 1, q],
            recv_sem=recv_sem.at[o - 1, q],
            device_id={"comp": target},
            device_id_type=mesh_id,
        )

    def remote_rest(o, source, target):
        return pltpu.make_async_remote_copy(
            src_ref=rest_send.at[target],
            dst_ref=rest_recv.at[source],
            send_sem=rest_ssem.at[o - 1],
            recv_sem=rest_rsem.at[o - 1],
            device_id={"comp": target},
            device_id_type=mesh_id,
        )

    def spread_chunk(q):
        @pl.loop(0, PAIR * (main // PACK))
        def _(i):
            start = pl.multiple_of(lax.rem(i, main // PACK) * PACK, PACK)
            upwind(q * PAIR + i // (main // PACK), start, False)

        for o in range(1, n):
            remote(q, o, me, lax.rem(me + o, n)).start()
        here = pl.ds(q * PAIR, PAIR)
        recv[me, here] = send[me, here]

    turn_in(0, True)
    pl.semaphore_wait(barrier, devices - 1)
    spread_chunk(jnp.int32(1))
    last_quarter = rows // QUARTER - 1
    turn_in(last_quarter, True)

    to_below = pltpu.make_async_remote_copy(
        src_ref=xs.at[pl.ds(rows, 1)],
        dst_ref=xs.at[pl.ds(0, 1)],
        send_sem=z_send.at[0],
        recv_sem=z_recv.at[0],
        device_id=below,
        device_id_type=mesh_id,
    )
    to_above = pltpu.make_async_remote_copy(
        src_ref=xs.at[pl.ds(1, 1)],
        dst_ref=xs.at[pl.ds(rows + 1, 1)],
        send_sem=z_send.at[1],
        recv_sem=z_recv.at[1],
        device_id=above,
        device_id_type=mesh_id,
    )

    @pl.when(jnp.logical_not(is_bottom))
    def _():
        to_below.start()

    @pl.when(jnp.logical_not(is_top))
    def _():
        to_above.start()

    for c in range(1, last_quarter):
        turn_in(c, c % 2 == 0 and c != last_quarter - 1)

    per_quarter = QUARTER // PAIR

    @pl.loop(2, per_quarter)
    def _(q):
        spread_chunk(q)

    for i in range(2, len(smalls)):
        small(i).wait()

    lane_d = lax.broadcasted_iota(jnp.int32, (devices, LANES), 0)
    up_to = lax.broadcasted_iota(jnp.int32, (LANES, 2 * LANES), 0)
    at = lax.broadcasted_iota(jnp.int32, (LANES, 2 * LANES), 1)
    counting = jnp.where(jnp.logical_or(up_to < at, at >= LANES), 1.0, 0.0).astype(BF16)
    base[...] = jnp.zeros(base.shape, F32)

    @pl.loop(0, rows)
    def _(r):
        hit = jnp.where(owner[pl.ds(r, 1), :] == lane_d, 1.0, 0.0)
        counts = jnp.dot(hit.astype(BF16), counting, preferred_element_type=F32)
        before = hit * (counts[:, :LANES] + base[...])
        rank[pl.ds(r, 1), :] = jnp.sum(before, axis=0, keepdims=True).astype(jnp.int32)
        base[...] += counts[:, LANES:]

    sub = lax.broadcasted_iota(jnp.int32, (PACK, LANES), 0)
    slot_lane = lax.broadcasted_iota(jnp.int32, (LANES, LANES), 0)
    owner_of = lax.broadcasted_iota(jnp.int32, (devices, PACK, LANES), 0)

    def pack(row, items):
        place = rank[pl.ds(row, 1), :]
        block, lane = place // LANES, lax.rem(place, LANES)
        rows_of = jnp.zeros((PACK, LANES), F32)
        for f in range(len(items)):
            for b in range(nb):
                here = jnp.logical_and(sub == f * nb + b, block == b)
                rows_of = jnp.where(here, items[f], rows_of)
        mine = owner[pl.ds(row, 1), :][None] == owner_of
        spread = jnp.where(mine, rows_of[None], 0.0).astype(BF16)
        onehot = jnp.where(lane == slot_lane, 1.0, 0.0).astype(BF16)
        return spread.reshape(devices * PACK, LANES), onehot

    def pack_pair(row, items):
        halves_of = [pack(row + a, items[a]) for a in range(PAIR)]
        packed_acc[...] += nt_dot(
            jnp.concatenate([h[0] for h in halves_of], axis=1),
            jnp.concatenate([h[1] for h in halves_of], axis=1),
        )

    def route(which, o, source, target):
        return pltpu.make_async_remote_copy(
            src_ref=packed.at[which, target],
            dst_ref=got.at[which, source],
            send_sem=route_ssem.at[which, o - 1],
            recv_sem=route_rsem.at[which, o - 1],
            device_id={"comp": target // n_tile, "tile": lax.rem(target, n_tile)},
            device_id_type=mesh_id,
        )

    def send_packed(which):
        packed[which] = packed_acc[...].astype(BF16).reshape(devices, PACK, LANES)

        @pl.loop(1, devices)
        def _(o):
            route(which, o, number, lax.rem(number + o, devices)).start()

        got[which, number] = packed[which, number]

    def wait_packed(which):
        @pl.loop(1, devices)
        def _(o):
            route(which, o, lax.rem(number + devices - o, devices), number).wait_recv()

    packed_acc[...] = jnp.zeros(packed_acc.shape, F32)

    @pl.loop(0, steps)
    def _(i):
        items = []
        for a in range(PAIR):
            c = cell[pl.ds(i * PAIR + a, 1), :]
            items.append([(c // cells_c).astype(F32), lax.rem(c, cells_c).astype(F32)])
        pack_pair(i * PAIR, items)

    send_packed(0)
    @pl.when(jnp.logical_not(is_top))
    def _():
        to_below.wait_recv()

    @pl.when(jnp.logical_not(is_bottom))
    def _():
        to_above.wait_recv()

    if rest:

        @pl.loop(0, rows)
        def _(i):
            upwind(i, main, True)

    if rest:
        rest_send[...] = rest_f[...].astype(BF16)
        for o in range(1, n):
            remote_rest(o, me, lax.rem(me + o, n)).start()
        rest_recv[me] = rest_send[me]

    spread_chunk(jnp.int32(0))

    @pl.loop(per_quarter, steps)
    def _(q):
        spread_chunk(q)

    to_columns(dissipation, 0)
    to_columns(growth, 1)
    columns[...] = WAVE_STEP * columns[...]

    packed_acc[...] = jnp.zeros(packed_acc.shape, F32)

    get_table.wait()
    bin_high, bin_low = split_two(bins[...].reshape(1, full))
    which = lax.broadcasted_iota(jnp.int32, (PACK, full), 0)
    table[full : full + PACK, :] = jnp.where(
        which == 0, bin_high.astype(F32), jnp.where(which == 1, bin_low.astype(F32), 0.0)
    ).astype(BF16)
    orbit = split_two(orbital[...].reshape(1, full))
    push = split_two(stress[...])
    weight = jnp.zeros((PACK, full), F32)
    for half in range(2):
        lines = [push[half][0:1], push[half][1:2], orbit[half]]
        for f in range(3):
            weight = jnp.where(which == 3 * half + f, lines[f].astype(F32), weight)
    weights[...] = weight.astype(BF16)

    band = 3 * PACK if full % (3 * PACK) == 0 else PACK

    def mix(q):
        row = q * PAIR
        for s in range(n):
            for a in range(PAIR):
                span = slice(a * cols, (a + 1) * cols)
                whole[s * own : s * own + main, span] = recv[s, row + a].astype(F32)
                if rest:
                    whole[s * own + main : (s + 1) * own, span] = rest_f[
                        s, pl.ds((row + a) * rest, rest), :
                    ]
        acc[...] = jnp.dot(table[...], whole[...].astype(BF16), preferred_element_type=F32)
        total = acc[full : full + 1, :] + acc[full + 1 : full + 2, :]
        ratio = total / (total + 1.0)
        gust = jnp.concatenate([wind[pl.ds(row + a, 1), :] for a in range(PAIR)], axis=1)
        open_water = jnp.concatenate(
            [wet[pl.ds(row + a, 1), :].astype(F32) for a in range(PAIR)], axis=1
        )
        spot = lax.rem(row, QUARTER)

        @pl.loop(0, full // band)
        def _(b):
            part = pl.ds(pl.multiple_of(b * band, band), band)
            damping, growing = columns[0, part, :], columns[1, part, :]
            for a in range(PAIR):
                span = slice(a * cols, (a + 1) * cols)
                gain = 1.0 - damping * ratio[:, span] + growing * gust[:, span]
                relaxed = WAVE_STEP * acc[part, span] + whole[part, span] * gain
                fresh = open_water[:, span] * jnp.maximum(relaxed, 0.0)
                stage[spot + a, part, :] = fresh.astype(BF16)

        fresh_all = jnp.concatenate([stage[spot + a] for a in range(PAIR)], axis=1)
        pulled = jnp.dot(weights[...], fresh_all, preferred_element_type=F32)
        forces = pulled[0:3] + pulled[3:6]
        pack_pair(
            row,
            [
                [forces[f : f + 1, a * cols : (a + 1) * cols] for f in range(3)]
                for a in range(PAIR)
            ],
        )

    def mix_step(q):
        for o in range(1, n):
            remote(q, o, lax.rem(me + n - o, n), me).wait_recv()
        mix(q)

    def turn_out(c):
        @pl.loop(0, full // PACK)
        def _(g):
            part = pl.ds(pl.multiple_of(g * PACK, PACK), PACK)
            block = stage[:, part, :].astype(F32)
            out[part, c * QUARTER : (c + 1) * QUARTER, :] = jnp.swapaxes(block, 0, 1).astype(BF16)

    if rest:
        for o in range(1, n):
            remote_rest(o, lax.rem(me + n - o, n), me).wait_recv()
        rest_f[...] = rest_recv[...].astype(F32)

    @pl.loop(0, per_quarter)
    def _(step):
        mix_step(lax.rem(step + 1, per_quarter))

    turn_out(0)

    for c in range(1, rows // QUARTER):
        if c == last_quarter:
            wait_packed(0)

            @pl.loop(0, devices)
            def _(s):
                cells = got[0, s].astype(F32)
                for b in range(nb):
                    spot = pl.ds(pl.multiple_of((s * nb + b) * LANES, LANES), LANES)
                    col = cells[nb + b : nb + b + 1, :]
                    targets[:, spot] = jnp.where(col == slot_lane.astype(F32), 1.0, 0.0).astype(BF16)

        @pl.loop(c * per_quarter, (c + 1) * per_quarter)
        def _(q):
            mix_step(q)

        if c == last_quarter:
            send_packed(1)
        turn_out(c)

    wait_packed(1)
    cell_row = lax.broadcasted_iota(jnp.int32, (cells_r, LANES), 0).astype(F32)

    bottom = jnp.zeros((3 * cells_r, cells_c), F32)
    share = devices // PARTS
    for start in range(0, devices, share):

        @pl.loop(0, share)
        def _(i):
            cells = got[0, start + i].astype(F32)
            force = got[1, start + i].astype(F32)
            for b in range(nb):
                spot = pl.ds(pl.multiple_of((i * nb + b) * LANES, LANES), LANES)
                hit = cells[b : b + 1, :] == cell_row
                for f in range(3):
                    lifted[f * cells_r : (f + 1) * cells_r, spot] = jnp.where(
                        hit, force[f * nb + b : f * nb + b + 1, :], 0.0
                    ).astype(BF16)

        these = slice(start * nb * LANES, (start + share) * nb * LANES)
        bottom += nt_dot(lifted[...], targets[:, these])

    shear_x = current[0] + bottom[0:cells_r]
    shear_y = current[1] + bottom[cells_r : 2 * cells_r]
    shear = jnp.sqrt(shear_x * shear_x + shear_y * shear_y + bottom[2 * cells_r :])
    classes = sediment.shape[0]
    count = classes + metals.shape[0]
    low_share = 0.5 / classes
    high_share = 1.0 - (classes - 1) * low_share
    wetness = roms[...].astype(F32)
    for s in range(classes):
        fraction = jnp.where(bed[...] == s, high_share, low_share)
        rate, critical, settling = [props[i : i + 1, s : s + 1] for i in range(3)]
        erosion = rate * fraction * jnp.maximum(shear / critical - 1.0, 0.0)
        here = sediment[s]
        fields[s] = wetness * (here + SEDIMENT_STEP * (erosion - settling * here))
    for m in range(count - classes):
        fields[classes + m] = wetness * metals[m]

    held = fields[...]
    edge_s[0] = held[:, cells_r - 1, :]
    edge_s[1] = held[:, 0, :]
    turned = held.reshape(count * cells_r, cells_c).T
    edge_s[2, 0:1, :] = turned[cells_c - 1 :]
    edge_s[3, 0:1, :] = turned[0:1]

    def halo(i, device):
        return pltpu.make_async_remote_copy(
            src_ref=edge_s.at[i],
            dst_ref=edge_r.at[i],
            send_sem=halo_ssem.at[i],
            recv_sem=halo_rsem.at[i],
            device_id=device,
            device_id_type=mesh_id,
        )

    halos = [halo(0, below), halo(1, above), halo(2, east_of), halo(3, west_of)]
    sends = [is_bottom, is_top, is_right, is_left]
    receives = [is_top, is_bottom, is_left, is_right]
    for i in range(4):
        pl.when(jnp.logical_not(sends[i]))(halos[i].start)
    for i in range(4):
        pl.when(jnp.logical_not(receives[i]))(halos[i].wait_recv)

    north = jnp.concatenate([edge_r[0][:, None, :], held[:, :-1, :]], axis=1)
    south = jnp.concatenate([held[:, 1:, :], edge_r[1][:, None, :]], axis=1)
    flat = held.reshape(count * cells_r, cells_c)
    lane = lax.broadcasted_iota(jnp.int32, flat.shape, 1)

    def column(i):
        return jnp.broadcast_to(edge_r[i, 0:1, :], (cells_c, count * cells_r)).T

    west = jnp.where(lane == 0, column(2), pltpu.roll(flat, 1, 1)).reshape(held.shape)
    east = jnp.where(lane == cells_c - 1, column(3), pltpu.roll(flat, cells_c - 1, 1)).reshape(
        held.shape
    )
    beside = north + south + west + east
    result[...] = wetness[None] * (held + DIFFUSION * (beside - 4.0 * held))

    for i in range(4):
        pl.when(jnp.logical_not(sends[i]))(halos[i].wait_send)
    pl.when(jnp.logical_not(is_bottom))(to_below.wait_send)
    pl.when(jnp.logical_not(is_top))(to_above.wait_send)

    @pl.loop(0, steps)
    def _(q):
        for o in range(1, n):
            remote(q, o, me, lax.rem(me + o, n)).wait_send()

    if rest:
        for o in range(1, n):
            remote_rest(o, me, lax.rem(me + o, n)).wait_send()

    @pl.loop(1, devices)
    def _(o):
        for which in range(2):
            route(which, o, number, lax.rem(number + o, devices)).wait_send()


def on_device(
    spectrum,
    courant_x,
    courant_y,
    growth,
    dissipation,
    bin_width,
    transfer,
    stress_weights,
    orbital_weights,
    wind,
    wave_wet,
    owner,
    cell_index,
    current_stress,
    sediment,
    metals,
    bed_class,
    roms_wet,
    class_props,
    partition,
):
    n = lax.axis_size("comp")
    n_tile = lax.axis_size("tile")
    devices = n * n_tile
    own, rows, width = spectrum.shape
    cols = width // n
    full = n * own
    main = own // PACK * PACK
    rest = own - main
    padded = main + (PACK if rest else 0)
    rest_rows = max(rest, 1) * rows
    slots = max(2, 3 * rows * cols // devices)
    nb = -(-slots // LANES)
    steps = rows // PAIR
    classes, cells_r, cells_c = sediment.shape
    count = classes + metals.shape[0]

    operands = (
        spectrum,
        courant_x,
        courant_y,
        growth,
        dissipation,
        bin_width,
        transfer,
        stress_weights,
        orbital_weights,
        wind,
        wave_wet,
        owner.reshape(rows, cols),
        cell_index.reshape(rows, cols),
        current_stress,
        sediment,
        metals,
        bed_class,
        roms_wet,
        class_props,
    )
    vmem = pl.BlockSpec(memory_space=pltpu.VMEM)
    hbm = pl.BlockSpec(memory_space=pltpu.HBM)

    def like(i):
        return pltpu.VMEM(operands[i].shape, operands[i].dtype)

    dma = pltpu.SemaphoreType.DMA
    scratch = [
        *[like(i) for i in range(1, 6)],
        pltpu.VMEM((full + PACK, full), BF16),
        *[like(i) for i in range(7, len(operands))],
        pltpu.VMEM((2, full, LANES), F32),
        pltpu.VMEM((5, padded, cols), F32),
        pltpu.VMEM((rows + 2, padded, width), BF16),
        pltpu.VMEM((n, rows, main, cols), BF16),
        pltpu.VMEM((n, rows, main, cols), BF16),
        pltpu.VMEM((n, rest_rows, cols), F32),
        pltpu.VMEM((n, rest_rows, cols), BF16),
        pltpu.VMEM((n, rest_rows, cols), BF16),
        pltpu.VMEM((full, PAIR * cols), F32),
        pltpu.VMEM((full + PACK, PAIR * cols), F32),
        pltpu.VMEM((QUARTER, full, cols), BF16),
        pltpu.VMEM((PACK, full), BF16),
        pltpu.VMEM((rows, cols), jnp.int32),
        pltpu.VMEM((devices, LANES), F32),
        pltpu.VMEM((devices * PACK, LANES), F32),
        pltpu.VMEM((2, devices, PACK, LANES), BF16),
        pltpu.VMEM((2, devices, PACK, LANES), BF16),
        pltpu.VMEM((LANES, devices * nb * LANES), BF16),
        pltpu.VMEM((3 * cells_r, devices // PARTS * nb * LANES), BF16),
        pltpu.VMEM((count, cells_r, cells_c), F32),
        pltpu.VMEM((4, count, cells_c), F32),
        pltpu.VMEM((4, count, cells_c), F32),
        dma((len(operands),)),
        dma((rows // PACK, n)),
        dma((1,)),
        dma((2,)),
        dma((2,)),
        dma((n - 1, steps)),
        dma((n - 1, steps)),
        dma((n - 1,)),
        dma((n - 1,)),
        dma((2, devices - 1)),
        dma((2, devices - 1)),
        dma((4,)),
        dma((4,)),
    ]
    fresh, diffused = pl.pallas_call(
        functools.partial(step_kernel, n, n_tile, slots),
        out_shape=(
            pltpu.VMEM((full, rows, cols), BF16),
            pltpu.VMEM((count, cells_r, cells_c), F32),
        ),
        in_specs=[hbm] * len(operands),
        out_specs=(vmem, vmem),
        scratch_shapes=scratch,
        compiler_params=pltpu.CompilerParams(
            collective_id=0, has_side_effects=True, vmem_limit_bytes=54000 * 1024
        ),
    )(*operands)

    sediment_new = diffused[:classes]
    spread = diffused[classes:]
    denominator = 1.0 + jnp.sum(partition[:, :, None, None] * sediment_new[None], axis=1)
    dissolved = spread / denominator
    return (fresh, sediment_new, dissolved, spread - dissolved)


def solution(mesh):
    replicated = P()
    grid = P("tile", "comp")
    fields = P(None, "tile", "comp")
    in_specs = (
        P("comp", "tile", None),
        *[replicated] * 8,
        grid,
        grid,
        P("tile", "comp", None, None, None),
        P("tile", "comp", None, None),
        fields,
        fields,
        fields,
        grid,
        grid,
        replicated,
        replicated,
    )
    return jax.shard_map(
        on_device, mesh=mesh, in_specs=in_specs, out_specs=(fields,) * 4, check_vma=False
    )
```

```python
import functools

import jax
import jax.numpy as jnp
from jax import lax
from jax.experimental import pallas as pl
from jax.experimental.pallas import tpu as pltpu
from jax.sharding import PartitionSpec as P

WAVE_STEP = 0.5
SEDIMENT_STEP = 1.0
DIFFUSION = 0.2
LANES = 128
PACK = 16
PAIR = 2
QUARTER = 8
SHARE = 32
PIECES = 8
F32 = jnp.float32
BF16 = jnp.bfloat16


def nt_dot(a, b):
    return lax.dot_general(a, b, (((1,), (1,)), ((), ())), preferred_element_type=F32)


def split_two(values):
    high = values.astype(BF16)
    return high, (values - high.astype(F32)).astype(BF16)


def step_kernel(
    n,
    n_tile,
    slots,
    x_hbm,
    cx_hbm,
    cy_hbm,
    grow_hbm,
    damp_hbm,
    bin_hbm,
    transfer_hbm,
    stress_hbm,
    orbital_hbm,
    wind_hbm,
    wet_hbm,
    owner_hbm,
    cell_hbm,
    current_hbm,
    sediment_hbm,
    metals_hbm,
    bed_hbm,
    roms_hbm,
    props_hbm,
    out,
    result,
    cx,
    cy,
    growth,
    dissipation,
    bins,
    table,
    stress,
    orbital,
    wind,
    wet,
    owner,
    cell,
    current,
    sediment,
    metals,
    bed,
    roms,
    props,
    columns,
    coef,
    xs,
    send,
    recv,
    rest_f,
    rest_send,
    rest_recv,
    whole,
    acc,
    stage,
    weights,
    rank,
    base,
    packed_acc,
    packed,
    got,
    targets,
    lifted,
    fields,
    edge_s,
    edge_r,
    small_sem,
    in_sem,
    table_sem,
    z_send,
    z_recv,
    send_sem,
    recv_sem,
    rest_ssem,
    rest_rsem,
    route_ssem,
    route_rsem,
    halo_ssem,
    halo_rsem,
):
    me = lax.axis_index("comp")
    tile = lax.axis_index("tile")
    devices = n * n_tile
    number = me * n_tile + tile
    own, rows, width = x_hbm.shape
    cols = width // n
    full = n * own
    main = own // PACK * PACK
    rest = own - main
    groups = main // PACK + (1 if rest else 0)
    steps = rows // PAIR
    halves = rows // PACK
    nb = -(-slots // LANES)
    cells_r, cells_c = result.shape[1], result.shape[2]
    is_top, is_bottom = tile == 0, tile == n_tile - 1
    is_left, is_right = me == 0, me == n - 1
    mesh_id = pl.DeviceIdType.MESH
    above = {"tile": lax.rem(tile + n_tile - 1, n_tile)}
    below = {"tile": lax.rem(tile + 1, n_tile)}
    west_of = {"comp": lax.rem(me + n - 1, n)}
    east_of = {"comp": lax.rem(me + 1, n)}

    barrier = pltpu.get_barrier_semaphore()

    @pl.loop(1, devices)
    def _(o):
        t = lax.rem(number + o, devices)
        pl.semaphore_signal(
            barrier,
            inc=1,
            device_id={"comp": t // n_tile, "tile": lax.rem(t, n_tile)},
            device_id_type=mesh_id,
        )

    smalls = [
        (cx_hbm, cx),
        (cy_hbm, cy),
        (bin_hbm, bins),
        (stress_hbm, stress),
        (orbital_hbm, orbital),
        (grow_hbm, growth),
        (damp_hbm, dissipation),
        (wind_hbm, wind),
        (wet_hbm, wet),
        (owner_hbm, owner),
        (cell_hbm, cell),
        (current_hbm, current),
        (sediment_hbm, sediment),
        (metals_hbm, metals),
        (bed_hbm, bed),
        (roms_hbm, roms),
        (props_hbm, props),
    ]

    def small(i):
        return pltpu.make_async_copy(smalls[i][0], smalls[i][1], small_sem.at[i])

    def load(h, d):
        return pltpu.make_async_copy(
            x_hbm.at[:, pl.ds(h * PACK, PACK), pl.ds(d * cols, cols)],
            out.at[pl.ds(d * own, own), pl.ds(h * PACK, PACK), :],
            in_sem.at[h],
        )

    def loaded(h):
        block = out.at[:, pl.ds(h * PACK, PACK), :]
        return pltpu.make_async_copy(block, block, in_sem.at[h])

    def all_of(block, sem):
        return pltpu.make_async_copy(block, block, sem)

    small(0).start()
    small(1).start()
    for h in range(halves):
        for d in range(n):
            load(h, d).start()
    for i in range(2, len(smalls)):
        small(i).start()
    get_table = pltpu.make_async_copy(transfer_hbm, table.at[pl.ds(0, full)], table_sem.at[0])
    get_table.start()

    def to_columns(values, i):
        for b in range(0, full, LANES):
            size = min(LANES, full - b)
            line = values[pl.ds(b, size)].reshape(1, size)
            columns[i, b : b + size, :] = jnp.broadcast_to(line, (LANES, size)).T

    small(0).wait()
    small(1).wait()
    to_columns(cx, 0)
    to_columns(cy, 1)

    for g in range(groups):
        first = g * PACK if g * PACK < main else own - PACK
        speed_x = columns[0, pl.ds(me * own + first, PACK), :]
        speed_y = columns[1, pl.ds(me * own + first, PACK), :]
        part = slice(g * PACK, (g + 1) * PACK)
        coef[0, part, :] = 1.0 - jnp.abs(speed_x) - jnp.abs(speed_y)
        coef[1, part, :] = jnp.maximum(speed_x, 0.0)
        coef[2, part, :] = -jnp.minimum(speed_x, 0.0)
        coef[3, part, :] = jnp.maximum(speed_y, 0.0)
        coef[4, part, :] = -jnp.minimum(speed_y, 0.0)

    @pl.when(is_top)
    def _():
        xs[0] = jnp.zeros(xs.shape[1:], BF16)
        edge_r[0] = jnp.zeros(edge_r.shape[1:], F32)

    @pl.when(is_bottom)
    def _():
        xs[rows + 1] = jnp.zeros(xs.shape[1:], BF16)
        edge_r[1] = jnp.zeros(edge_r.shape[1:], F32)

    @pl.when(is_left)
    def _():
        edge_r[2] = jnp.zeros(edge_r.shape[1:], F32)

    @pl.when(is_right)
    def _():
        edge_r[3] = jnp.zeros(edge_r.shape[1:], F32)

    def turn_in(c, is_first):
        top = c * QUARTER
        if is_first:
            loaded(top // PACK).wait()
        for d in range(n):

            def piece(at, first):
                block = out[pl.ds(d * own + first, PACK), top : top + QUARTER, :].astype(F32)
                xs[1 + top : 1 + top + QUARTER, pl.ds(at, PACK), d * cols : (d + 1) * cols] = (
                    jnp.swapaxes(block, 0, 1).astype(BF16)
                )

            @pl.loop(0, main // PACK)
            def _(g):
                start = pl.multiple_of(g * PACK, PACK)
                piece(start, start)

            if rest:
                piece(main, own - PACK)

    def upwind(row, start, is_rest):
        part = pl.ds(start, PACK)
        lane = lax.broadcasted_iota(jnp.int32, (PACK, cols), 1)
        first_lane, last_lane = lane == 0, lane == cols - 1
        kept, from_north, from_south, from_west, from_east = [coef[i, part, :] for i in range(5)]

        def tile_of(at, d):
            return xs[at, part, d * cols : (d + 1) * cols].astype(F32)

        centre = [tile_of(row + 1, d) for d in range(n)]
        right = [pltpu.roll(c, 1, 1) for c in centre]
        left = [pltpu.roll(c, cols - 1, 1) for c in centre]
        nothing = jnp.zeros((PACK, cols), F32)
        for d in range(n):
            west = jnp.where(first_lane, right[d - 1] if d else nothing, right[d])
            east = jnp.where(last_lane, left[d + 1] if d < n - 1 else nothing, left[d])
            moved = (
                kept * centre[d]
                + from_north * tile_of(row, d)
                + from_south * tile_of(row + 2, d)
                + from_west * west
                + from_east * east
            )
            if is_rest:
                rest_f[d, pl.ds(row * rest, rest), :] = moved[PACK - rest :]
            else:
                send[d, row, part, :] = moved.astype(BF16)

    def remote(q, o, source, target):
        return pltpu.make_async_remote_copy(
            src_ref=send.at[target, pl.ds(q * PAIR, PAIR)],
            dst_ref=recv.at[source, pl.ds(q * PAIR, PAIR)],
            send_sem=send_sem.at[0],
            recv_sem=recv_sem.at[q],
            device_id={"comp": target},
            device_id_type=mesh_id,
        )

    def remote_rest(o, source, target):
        return pltpu.make_async_remote_copy(
            src_ref=rest_send.at[target],
            dst_ref=rest_recv.at[source],
            send_sem=rest_ssem.at[0],
            recv_sem=rest_rsem.at[0],
            device_id={"comp": target},
            device_id_type=mesh_id,
        )

    def spread_chunk(q):
        @pl.loop(0, PAIR * (main // PACK))
        def _(i):
            start = pl.multiple_of(lax.rem(i, main // PACK) * PACK, PACK)
            upwind(q * PAIR + i // (main // PACK), start, False)

        for o in range(1, n):
            remote(q, o, me, lax.rem(me + o, n)).start()
        here = pl.ds(q * PAIR, PAIR)
        recv[me, here] = send[me, here]

    turn_in(0, True)
    pl.semaphore_wait(barrier, devices - 1)
    spread_chunk(jnp.int32(1))
    last_quarter = rows // QUARTER - 1
    turn_in(last_quarter, True)

    to_below = pltpu.make_async_remote_copy(
        src_ref=xs.at[pl.ds(rows, 1)],
        dst_ref=xs.at[pl.ds(0, 1)],
        send_sem=z_send.at[0],
        recv_sem=z_recv.at[0],
        device_id=below,
        device_id_type=mesh_id,
    )
    to_above = pltpu.make_async_remote_copy(
        src_ref=xs.at[pl.ds(1, 1)],
        dst_ref=xs.at[pl.ds(rows + 1, 1)],
        send_sem=z_send.at[1],
        recv_sem=z_recv.at[1],
        device_id=above,
        device_id_type=mesh_id,
    )

    @pl.when(jnp.logical_not(is_bottom))
    def _():
        to_below.start()

    @pl.when(jnp.logical_not(is_top))
    def _():
        to_above.start()

    for c in range(1, last_quarter):
        turn_in(c, c % 2 == 0 and c != last_quarter - 1)

    per_quarter = QUARTER // PAIR

    @pl.loop(2, per_quarter)
    def _(q):
        spread_chunk(q)

    @pl.when(jnp.logical_not(is_top))
    def _():
        to_below.wait_recv()

    @pl.when(jnp.logical_not(is_bottom))
    def _():
        to_above.wait_recv()

    if rest:

        @pl.loop(0, rows)
        def _(i):
            upwind(i, main, True)

    if rest:
        rest_send[...] = rest_f[...].astype(BF16)
        for o in range(1, n):
            remote_rest(o, me, lax.rem(me + o, n)).start()
        rest_recv[me] = rest_send[me]

    spread_chunk(jnp.int32(0))

    @pl.loop(per_quarter, 2 * per_quarter)
    def _(q):
        spread_chunk(q)

    for i in range(2, len(smalls)):
        small(i).wait()

    lane_d = lax.broadcasted_iota(jnp.int32, (devices, LANES), 0)
    up_to = lax.broadcasted_iota(jnp.int32, (LANES, 2 * LANES), 0)
    at = lax.broadcasted_iota(jnp.int32, (LANES, 2 * LANES), 1)
    counting = jnp.where(jnp.logical_or(up_to < at, at >= LANES), 1.0, 0.0).astype(BF16)
    base[...] = jnp.zeros(base.shape, F32)

    @pl.loop(0, rows)
    def _(r):
        hit = jnp.where(owner[pl.ds(r, 1), :] == lane_d, 1.0, 0.0)
        counts = jnp.dot(hit.astype(BF16), counting, preferred_element_type=F32)
        before = hit * (counts[:, :LANES] + base[...])
        rank[pl.ds(r, 1), :] = jnp.sum(before, axis=0, keepdims=True).astype(jnp.int32)
        base[...] += counts[:, LANES:]

    sub = lax.broadcasted_iota(jnp.int32, (PACK, LANES), 0)
    slot_lane = lax.broadcasted_iota(jnp.int32, (LANES, LANES), 0)
    owner_of = lax.broadcasted_iota(jnp.int32, (devices, PACK, LANES), 0)

    def pack(row, items):
        place = rank[pl.ds(row, 1), :]
        block, lane = place // LANES, lax.rem(place, LANES)
        rows_of = jnp.zeros((PACK, LANES), F32)
        for f in range(len(items)):
            for b in range(nb):
                here = jnp.logical_and(sub == f * nb + b, block == b)
                rows_of = jnp.where(here, items[f], rows_of)
        mine = owner[pl.ds(row, 1), :][None] == owner_of
        spread = jnp.where(mine, rows_of[None], 0.0).astype(BF16)
        onehot = jnp.where(lane == slot_lane, 1.0, 0.0).astype(BF16)
        return spread.reshape(devices * PACK, LANES), onehot

    def pack_pair(row, items):
        halves_of = [pack(row + a, items[a]) for a in range(PAIR)]
        packed_acc[...] += nt_dot(
            jnp.concatenate([h[0] for h in halves_of], axis=1),
            jnp.concatenate([h[1] for h in halves_of], axis=1),
        )

    def route(which, o, source, target):
        return pltpu.make_async_remote_copy(
            src_ref=packed.at[which, target],
            dst_ref=got.at[which, source],
            send_sem=route_ssem.at[which],
            recv_sem=route_rsem.at[which],
            device_id={"comp": target // n_tile, "tile": lax.rem(target, n_tile)},
            device_id_type=mesh_id,
        )

    def send_packed(which):
        packed[which] = packed_acc[...].astype(BF16).reshape(devices, PACK, LANES)

        @pl.loop(1, devices)
        def _(o):
            route(which, o, number, lax.rem(number + o, devices)).start()

        got[which, number] = packed[which, number]

    def wait_packed(which):
        all_of(got.at[which, pl.ds(0, devices - 1)], route_rsem.at[which]).wait()

    packed_acc[...] = jnp.zeros(packed_acc.shape, F32)

    @pl.loop(0, steps)
    def _(i):
        items = []
        for a in range(PAIR):
            c = cell[pl.ds(i * PAIR + a, 1), :]
            items.append([(c // cells_c).astype(F32), lax.rem(c, cells_c).astype(F32)])
        pack_pair(i * PAIR, items)

    send_packed(0)
    @pl.loop(2 * per_quarter, steps)
    def _(q):
        spread_chunk(q)

    to_columns(dissipation, 0)
    to_columns(growth, 1)
    columns[...] = WAVE_STEP * columns[...]

    packed_acc[...] = jnp.zeros(packed_acc.shape, F32)

    get_table.wait()
    bin_high, bin_low = split_two(bins[...].reshape(1, full))
    which = lax.broadcasted_iota(jnp.int32, (PACK, full), 0)
    table[full : full + PACK, :] = jnp.where(
        which == 0, bin_high.astype(F32), jnp.where(which == 1, bin_low.astype(F32), 0.0)
    ).astype(BF16)
    orbit = split_two(orbital[...].reshape(1, full))
    push = split_two(stress[...])
    weight = jnp.zeros((PACK, full), F32)
    for half in range(2):
        lines = [push[half][0:1], push[half][1:2], orbit[half]]
        for f in range(3):
            weight = jnp.where(which == 3 * half + f, lines[f].astype(F32), weight)
    weights[...] = weight.astype(BF16)

    band = 3 * PACK if full % (3 * PACK) == 0 else PACK

    def mix(q):
        row = q * PAIR
        for s in range(n):
            for a in range(PAIR):
                span = slice(a * cols, (a + 1) * cols)
                whole[s * own : s * own + main, span] = recv[s, row + a].astype(F32)
                if rest:
                    whole[s * own + main : (s + 1) * own, span] = rest_f[
                        s, pl.ds((row + a) * rest, rest), :
                    ]
        acc[...] = jnp.dot(table[...], whole[...].astype(BF16), preferred_element_type=F32)
        total = acc[full : full + 1, :] + acc[full + 1 : full + 2, :]
        ratio = total / (total + 1.0)
        gust = jnp.concatenate([wind[pl.ds(row + a, 1), :] for a in range(PAIR)], axis=1)
        open_water = jnp.concatenate(
            [wet[pl.ds(row + a, 1), :].astype(F32) for a in range(PAIR)], axis=1
        )
        spot = lax.rem(row, QUARTER)

        @pl.loop(0, full // band)
        def _(b):
            part = pl.ds(pl.multiple_of(b * band, band), band)
            damping, growing = columns[0, part, :], columns[1, part, :]
            for a in range(PAIR):
                span = slice(a * cols, (a + 1) * cols)
                gain = 1.0 - damping * ratio[:, span] + growing * gust[:, span]
                relaxed = WAVE_STEP * acc[part, span] + whole[part, span] * gain
                fresh = open_water[:, span] * jnp.maximum(relaxed, 0.0)
                stage[spot + a, part, :] = fresh.astype(BF16)

        fresh_all = jnp.concatenate([stage[spot + a] for a in range(PAIR)], axis=1)
        pulled = jnp.dot(weights[...], fresh_all, preferred_element_type=F32)
        forces = pulled[0:3] + pulled[3:6]
        pack_pair(
            row,
            [
                [forces[f : f + 1, a * cols : (a + 1) * cols] for f in range(3)]
                for a in range(PAIR)
            ],
        )

    def mix_step(q):
        all_of(recv.at[pl.ds(0, n - 1), pl.ds(q * PAIR, PAIR)], recv_sem.at[q]).wait()
        mix(q)

    def turn_out(c):
        @pl.loop(0, full // PACK)
        def _(g):
            part = pl.ds(pl.multiple_of(g * PACK, PACK), PACK)
            block = stage[:, part, :].astype(F32)
            out[part, c * QUARTER : (c + 1) * QUARTER, :] = jnp.swapaxes(block, 0, 1).astype(BF16)

    if rest:
        all_of(rest_recv.at[pl.ds(0, n - 1)], rest_rsem.at[0]).wait()
        rest_f[...] = rest_recv[...].astype(F32)

    @pl.loop(0, per_quarter)
    def _(step):
        mix_step(lax.rem(step + 1, per_quarter))

    turn_out(0)

    for c in range(1, rows // QUARTER):
        if c == last_quarter:
            wait_packed(0)

            @pl.loop(0, devices)
            def _(s):
                cells = got[0, s].astype(F32)
                for b in range(nb):
                    spot = pl.ds(pl.multiple_of((s * nb + b) * LANES, LANES), LANES)
                    col = cells[nb + b : nb + b + 1, :]
                    targets[:, spot] = jnp.where(col == slot_lane.astype(F32), 1.0, 0.0).astype(BF16)

        @pl.loop(c * per_quarter, (c + 1) * per_quarter)
        def _(q):
            mix_step(q)

        if c == last_quarter:
            send_packed(1)
        turn_out(c)

    wait_packed(1)
    cell_row = lax.broadcasted_iota(jnp.int32, (cells_r, LANES), 0).astype(F32)

    bottom = jnp.zeros((3 * cells_r, cells_c), F32)
    share = min(devices, SHARE)
    for start in range(0, devices, share):

        @pl.loop(0, share)
        def _(i):
            cells = got[0, start + i].astype(F32)
            force = got[1, start + i].astype(F32)
            for b in range(nb):
                spot = pl.ds(pl.multiple_of((i * nb + b) * LANES, LANES), LANES)
                hit = cells[b : b + 1, :] == cell_row
                for f in range(3):
                    lifted[f * cells_r : (f + 1) * cells_r, spot] = jnp.where(
                        hit, force[f * nb + b : f * nb + b + 1, :], 0.0
                    ).astype(BF16)

        these = slice(start * nb * LANES, (start + share) * nb * LANES)
        bottom += nt_dot(lifted[...], targets[:, these])

    shear_x = current[0] + bottom[0:cells_r]
    shear_y = current[1] + bottom[cells_r : 2 * cells_r]
    shear = jnp.sqrt(shear_x * shear_x + shear_y * shear_y + bottom[2 * cells_r :])
    classes = sediment.shape[0]
    count = classes + metals.shape[0]
    low_share = 0.5 / classes
    high_share = 1.0 - (classes - 1) * low_share
    wetness = roms[...].astype(F32)
    for s in range(classes):
        fraction = jnp.where(bed[...] == s, high_share, low_share)
        rate, critical, settling = [props[i : i + 1, s : s + 1] for i in range(3)]
        erosion = rate * fraction * jnp.maximum(shear / critical - 1.0, 0.0)
        here = sediment[s]
        fields[s] = wetness * (here + SEDIMENT_STEP * (erosion - settling * here))
    for m in range(count - classes):
        fields[classes + m] = wetness * metals[m]

    held = fields[...]
    edge_s[0] = held[:, cells_r - 1, :]
    edge_s[1] = held[:, 0, :]
    turned = held.reshape(count * cells_r, cells_c).T
    edge_s[2, 0:1, :] = turned[cells_c - 1 :]
    edge_s[3, 0:1, :] = turned[0:1]

    def halo(i, device):
        return pltpu.make_async_remote_copy(
            src_ref=edge_s.at[i],
            dst_ref=edge_r.at[i],
            send_sem=halo_ssem.at[i],
            recv_sem=halo_rsem.at[i],
            device_id=device,
            device_id_type=mesh_id,
        )

    halos = [halo(0, below), halo(1, above), halo(2, east_of), halo(3, west_of)]
    sends = [is_bottom, is_top, is_right, is_left]
    receives = [is_top, is_bottom, is_left, is_right]
    for i in range(4):
        pl.when(jnp.logical_not(sends[i]))(halos[i].start)
    for i in range(4):
        pl.when(jnp.logical_not(receives[i]))(halos[i].wait_recv)

    north = jnp.concatenate([edge_r[0][:, None, :], held[:, :-1, :]], axis=1)
    south = jnp.concatenate([held[:, 1:, :], edge_r[1][:, None, :]], axis=1)
    flat = held.reshape(count * cells_r, cells_c)
    lane = lax.broadcasted_iota(jnp.int32, flat.shape, 1)

    def column(i):
        return jnp.broadcast_to(edge_r[i, 0:1, :], (cells_c, count * cells_r)).T

    west = jnp.where(lane == 0, column(2), pltpu.roll(flat, 1, 1)).reshape(held.shape)
    east = jnp.where(lane == cells_c - 1, column(3), pltpu.roll(flat, cells_c - 1, 1)).reshape(
        held.shape
    )
    beside = north + south + west + east
    result[...] = wetness[None] * (held + DIFFUSION * (beside - 4.0 * held))

    for i in range(4):
        pl.when(jnp.logical_not(sends[i]))(halos[i].wait_send)
    pl.when(jnp.logical_not(is_bottom))(to_below.wait_send)
    pl.when(jnp.logical_not(is_top))(to_above.wait_send)

    all_of(send.at[pl.ds(0, n - 1)], send_sem.at[0]).wait()
    if rest:
        all_of(rest_send.at[pl.ds(0, n - 1)], rest_ssem.at[0]).wait()
    for which in range(2):
        all_of(packed.at[which, pl.ds(0, devices - 1)], route_ssem.at[which]).wait()


def finish_kernel(
    fresh,
    diffused,
    partition,
    spectrum_hbm,
    sediment_hbm,
    dissolved_hbm,
    sorbed_hbm,
    dissolved,
    sorbed,
    big_sem,
    field_sem,
):
    full = fresh.shape[0]
    size = -(-full // PIECES)
    spans = [pl.ds(i, min(size, full - i)) for i in range(0, full, size)]
    copies = [
        pltpu.make_async_copy(fresh.at[span], spectrum_hbm.at[span], big_sem.at[i])
        for i, span in enumerate(spans)
    ]
    classes = sediment_hbm.shape[0]
    copies.append(
        pltpu.make_async_copy(diffused.at[pl.ds(0, classes)], sediment_hbm, field_sem.at[0])
    )
    for copy in copies:
        copy.start()
    for m in range(dissolved.shape[0]):
        denominator = 1.0 + sum(
            partition[m : m + 1, s : s + 1] * diffused[s] for s in range(classes)
        )
        spread = diffused[classes + m]
        quotient = spread / denominator
        dissolved[m] = quotient
        sorbed[m] = spread - quotient
    copies.append(pltpu.make_async_copy(dissolved, dissolved_hbm, field_sem.at[1]))
    copies.append(pltpu.make_async_copy(sorbed, sorbed_hbm, field_sem.at[2]))
    for copy in copies[-2:]:
        copy.start()
    for copy in copies:
        copy.wait()


def on_device(
    spectrum,
    courant_x,
    courant_y,
    growth,
    dissipation,
    bin_width,
    transfer,
    stress_weights,
    orbital_weights,
    wind,
    wave_wet,
    owner,
    cell_index,
    current_stress,
    sediment,
    metals,
    bed_class,
    roms_wet,
    class_props,
    partition,
):
    n = lax.axis_size("comp")
    n_tile = lax.axis_size("tile")
    devices = n * n_tile
    own, rows, width = spectrum.shape
    cols = width // n
    full = n * own
    main = own // PACK * PACK
    rest = own - main
    padded = main + (PACK if rest else 0)
    rest_rows = max(rest, 1) * rows
    slots = max(2, 3 * rows * cols // devices)
    nb = -(-slots // LANES)
    steps = rows // PAIR
    classes, cells_r, cells_c = sediment.shape
    count = classes + metals.shape[0]

    operands = (
        spectrum,
        courant_x,
        courant_y,
        growth,
        dissipation,
        bin_width,
        transfer,
        stress_weights,
        orbital_weights,
        wind,
        wave_wet,
        owner.reshape(rows, cols),
        cell_index.reshape(rows, cols),
        current_stress,
        sediment,
        metals,
        bed_class,
        roms_wet,
        class_props,
    )
    vmem = pl.BlockSpec(memory_space=pltpu.VMEM)
    hbm = pl.BlockSpec(memory_space=pltpu.HBM)

    def like(i):
        return pltpu.VMEM(operands[i].shape, operands[i].dtype)

    dma = pltpu.SemaphoreType.DMA
    scratch = [
        *[like(i) for i in range(1, 6)],
        pltpu.VMEM((full + PACK, full), BF16),
        *[like(i) for i in range(7, len(operands))],
        pltpu.VMEM((2, full, LANES), F32),
        pltpu.VMEM((5, padded, cols), F32),
        pltpu.VMEM((rows + 2, padded, width), BF16),
        pltpu.VMEM((n, rows, main, cols), BF16),
        pltpu.VMEM((n, rows, main, cols), BF16),
        pltpu.VMEM((n, rest_rows, cols), F32),
        pltpu.VMEM((n, rest_rows, cols), BF16),
        pltpu.VMEM((n, rest_rows, cols), BF16),
        pltpu.VMEM((full, PAIR * cols), F32),
        pltpu.VMEM((full + PACK, PAIR * cols), F32),
        pltpu.VMEM((QUARTER, full, cols), BF16),
        pltpu.VMEM((PACK, full), BF16),
        pltpu.VMEM((rows, cols), jnp.int32),
        pltpu.VMEM((devices, LANES), F32),
        pltpu.VMEM((devices * PACK, LANES), F32),
        pltpu.VMEM((2, devices, PACK, LANES), BF16),
        pltpu.VMEM((2, devices, PACK, LANES), BF16),
        pltpu.VMEM((LANES, devices * nb * LANES), BF16),
        pltpu.VMEM((3 * cells_r, min(devices, SHARE) * nb * LANES), BF16),
        pltpu.VMEM((count, cells_r, cells_c), F32),
        pltpu.VMEM((4, count, cells_c), F32),
        pltpu.VMEM((4, count, cells_c), F32),
        dma((len(operands) - 2,)),
        dma((rows // PACK,)),
        dma((1,)),
        dma((2,)),
        dma((2,)),
        dma((1,)),
        dma((steps,)),
        dma((1,)),
        dma((1,)),
        dma((2,)),
        dma((2,)),
        dma((4,)),
        dma((4,)),
    ]
    fresh, diffused = pl.pallas_call(
        functools.partial(step_kernel, n, n_tile, slots),
        out_shape=(
            pltpu.VMEM((full, rows, cols), BF16),
            pltpu.VMEM((count, cells_r, cells_c), F32),
        ),
        in_specs=[hbm] * len(operands),
        out_specs=(vmem, vmem),
        scratch_shapes=scratch,
        compiler_params=pltpu.CompilerParams(
            collective_id=0, has_side_effects=True, vmem_limit_bytes=54000 * 1024
        ),
    )(*operands)

    field = jax.ShapeDtypeStruct((classes, cells_r, cells_c), F32)
    metal = jax.ShapeDtypeStruct((count - classes, cells_r, cells_c), F32)
    return tuple(
        pl.pallas_call(
            finish_kernel,
            out_shape=(jax.ShapeDtypeStruct(fresh.shape, fresh.dtype), field, metal, metal),
            in_specs=[pl.BlockSpec(memory_space=pl.ANY), vmem, vmem],
            out_specs=(hbm,) * 4,
            scratch_shapes=[
                pltpu.VMEM(metal.shape, F32),
                pltpu.VMEM(metal.shape, F32),
                dma((PIECES,)),
                dma((3,)),
            ],
            compiler_params=pltpu.CompilerParams(vmem_limit_bytes=4 << 20),
        )(
            pltpu.with_memory_space_constraint(fresh, pltpu.VMEM),
            pltpu.with_memory_space_constraint(diffused, pltpu.VMEM),
            partition,
        )
    )


def solution(mesh):
    replicated = P()
    grid = P("tile", "comp")
    fields = P(None, "tile", "comp")
    in_specs = (
        P("comp", "tile", None),
        *[replicated] * 8,
        grid,
        grid,
        P("tile", "comp", None, None, None),
        P("tile", "comp", None, None),
        fields,
        fields,
        fields,
        grid,
        grid,
        replicated,
        replicated,
    )
    return jax.shard_map(
        on_device, mesh=mesh, in_specs=in_specs, out_specs=(fields,) * 4, check_vma=False
    )
```

```python
import functools

import jax
import jax.numpy as jnp
from jax import lax
from jax.experimental import pallas as pl
from jax.experimental.pallas import tpu as pltpu
from jax.sharding import PartitionSpec as P

WAVE_STEP = 0.5
SEDIMENT_STEP = 1.0
DIFFUSION = 0.2
LANES = 128
PACK = 16
PAIR = 2
QUARTER = 8
SHARE = 32
PIECES = 8
F32 = jnp.float32
BF16 = jnp.bfloat16


def nt_dot(a, b):
    return lax.dot_general(a, b, (((1,), (1,)), ((), ())), preferred_element_type=F32)


def split_two(values):
    high = values.astype(BF16)
    return high, (values - high.astype(F32)).astype(BF16)


def step_kernel(
    n,
    n_tile,
    slots,
    x_hbm,
    cx_hbm,
    cy_hbm,
    grow_hbm,
    damp_hbm,
    bin_hbm,
    transfer_hbm,
    stress_hbm,
    orbital_hbm,
    wind_hbm,
    wet_hbm,
    owner_hbm,
    cell_hbm,
    current_hbm,
    sediment_hbm,
    metals_hbm,
    bed_hbm,
    roms_hbm,
    props_hbm,
    out,
    result,
    cx,
    cy,
    growth,
    dissipation,
    bins,
    table,
    stress,
    orbital,
    wind,
    wet,
    owner,
    cell,
    current,
    sediment,
    metals,
    bed,
    roms,
    props,
    columns,
    coef,
    xs,
    send,
    recv,
    rest_f,
    rest_send,
    rest_recv,
    whole,
    acc,
    stage,
    weights,
    rank,
    base,
    packed_acc,
    packed,
    got,
    targets,
    lifted,
    fields,
    edge_s,
    edge_r,
    small_sem,
    in_sem,
    table_sem,
    z_send,
    z_recv,
    send_sem,
    recv_sem,
    rest_ssem,
    rest_rsem,
    route_ssem,
    route_rsem,
    halo_ssem,
    halo_rsem,
):
    me = lax.axis_index("comp")
    tile = lax.axis_index("tile")
    devices = n * n_tile
    number = me * n_tile + tile
    own, rows, width = x_hbm.shape
    cols = width // n
    full = n * own
    main = own // PACK * PACK
    rest = own - main
    groups = main // PACK + (1 if rest else 0)
    steps = rows // PAIR
    halves = rows // PACK
    nb = -(-slots // LANES)
    cells_r, cells_c = result.shape[1], result.shape[2]
    is_top, is_bottom = tile == 0, tile == n_tile - 1
    is_left, is_right = me == 0, me == n - 1
    mesh_id = pl.DeviceIdType.MESH
    above = {"tile": lax.rem(tile + n_tile - 1, n_tile)}
    below = {"tile": lax.rem(tile + 1, n_tile)}
    west_of = {"comp": lax.rem(me + n - 1, n)}
    east_of = {"comp": lax.rem(me + 1, n)}

    def others(act):
        @pl.loop(0, n)
        def _(c):
            comp = lax.rem(me + c, n)
            for t in range(n_tile):
                if t:
                    act(comp, lax.rem(tile + t, n_tile))
                else:
                    pl.when(c > 0)(functools.partial(act, comp, tile))

    smalls = [
        (cx_hbm, cx),
        (cy_hbm, cy),
        (bin_hbm, bins),
        (stress_hbm, stress),
        (orbital_hbm, orbital),
        (grow_hbm, growth),
        (damp_hbm, dissipation),
        (wind_hbm, wind),
        (wet_hbm, wet),
        (owner_hbm, owner),
        (cell_hbm, cell),
        (current_hbm, current),
        (sediment_hbm, sediment),
        (metals_hbm, metals),
        (bed_hbm, bed),
        (roms_hbm, roms),
        (props_hbm, props),
    ]

    def small(i):
        return pltpu.make_async_copy(smalls[i][0], smalls[i][1], small_sem.at[i])

    cut = main // PACK // 2 * PACK
    parts = [(0, cut), (cut, own - cut)]

    def load(h, p, d):
        first, size = parts[p]
        return pltpu.make_async_copy(
            x_hbm.at[pl.ds(first, size), pl.ds(h * PACK, PACK), pl.ds(d * cols, cols)],
            out.at[pl.ds(d * own + first, size), pl.ds(h * PACK, PACK), :],
            in_sem.at[h, p],
        )

    def loaded(h, p):
        block = out.at[pl.ds(0, n * parts[p][1]), pl.ds(h * PACK, PACK), :]
        return pltpu.make_async_copy(block, block, in_sem.at[h, p])

    def all_of(block, sem):
        return pltpu.make_async_copy(block, block, sem)

    small(0).start()
    small(1).start()
    for p in range(2):
        for d in range(n):
            load(0, p, d).start()

    barrier = pltpu.get_barrier_semaphore()

    def greet(comp, at_tile):
        pl.semaphore_signal(
            barrier, inc=1, device_id={"comp": comp, "tile": at_tile}, device_id_type=mesh_id
        )

    others(greet)
    for h in range(1, halves):
        for p in range(2):
            for d in range(n):
                load(h, p, d).start()
    for i in range(2, len(smalls)):
        small(i).start()
    get_table = pltpu.make_async_copy(transfer_hbm, table.at[pl.ds(0, full)], table_sem.at[0])
    get_table.start()

    def to_columns(values, i):
        for b in range(0, full, LANES):
            size = min(LANES, full - b)
            line = values[pl.ds(b, size)].reshape(1, size)
            columns[i, b : b + size, :] = jnp.broadcast_to(line, (LANES, size)).T

    small(0).wait()
    small(1).wait()
    to_columns(cx, 0)
    to_columns(cy, 1)

    for g in range(groups):
        first = g * PACK if g * PACK < main else own - PACK
        speed_x = columns[0, pl.ds(me * own + first, PACK), :]
        speed_y = columns[1, pl.ds(me * own + first, PACK), :]
        part = slice(g * PACK, (g + 1) * PACK)
        coef[0, part, :] = 1.0 - jnp.abs(speed_x) - jnp.abs(speed_y)
        coef[1, part, :] = jnp.maximum(speed_x, 0.0)
        coef[2, part, :] = -jnp.minimum(speed_x, 0.0)
        coef[3, part, :] = jnp.maximum(speed_y, 0.0)
        coef[4, part, :] = -jnp.minimum(speed_y, 0.0)

    @pl.when(is_top)
    def _():
        xs[0] = jnp.zeros(xs.shape[1:], BF16)
        edge_r[0] = jnp.zeros(edge_r.shape[1:], F32)

    @pl.when(is_bottom)
    def _():
        xs[rows + 1] = jnp.zeros(xs.shape[1:], BF16)
        edge_r[1] = jnp.zeros(edge_r.shape[1:], F32)

    @pl.when(is_left)
    def _():
        edge_r[2] = jnp.zeros(edge_r.shape[1:], F32)

    @pl.when(is_right)
    def _():
        edge_r[3] = jnp.zeros(edge_r.shape[1:], F32)

    def turn_in(c, first_group, last_group, with_rest):
        top = c * QUARTER
        for d in range(n):

            def piece(at, first):
                block = out[pl.ds(d * own + first, PACK), top : top + QUARTER, :].astype(F32)
                xs[1 + top : 1 + top + QUARTER, pl.ds(at, PACK), d * cols : (d + 1) * cols] = (
                    jnp.swapaxes(block, 0, 1).astype(BF16)
                )

            @pl.loop(first_group, last_group)
            def _(g):
                start = pl.multiple_of(g * PACK, PACK)
                piece(start, start)

            if rest and with_rest:
                piece(main, own - PACK)

    def upwind(row, start, is_rest):
        part = pl.ds(start, PACK)
        lane = lax.broadcasted_iota(jnp.int32, (PACK, cols), 1)
        first_lane, last_lane = lane == 0, lane == cols - 1
        kept, from_north, from_south, from_west, from_east = [coef[i, part, :] for i in range(5)]

        def tile_of(at, d):
            return xs[at, part, d * cols : (d + 1) * cols].astype(F32)

        centre = [tile_of(row + 1, d) for d in range(n)]
        right = [pltpu.roll(c, 1, 1) for c in centre]
        left = [pltpu.roll(c, cols - 1, 1) for c in centre]
        nothing = jnp.zeros((PACK, cols), F32)
        for d in range(n):
            west = jnp.where(first_lane, right[d - 1] if d else nothing, right[d])
            east = jnp.where(last_lane, left[d + 1] if d < n - 1 else nothing, left[d])
            moved = (
                kept * centre[d]
                + from_north * tile_of(row, d)
                + from_south * tile_of(row + 2, d)
                + from_west * west
                + from_east * east
            )
            if is_rest:
                rest_f[d, pl.ds(row * rest, rest), :] = moved[PACK - rest :]
            else:
                send[d, row, part, :] = moved.astype(BF16)

    def remote(row, count, first, size, o):
        here = pl.ds(row, count), pl.ds(first, size)
        target = lax.rem(me + o, n)
        return pltpu.make_async_remote_copy(
            src_ref=send.at[target, *here],
            dst_ref=recv.at[me, *here],
            send_sem=send_sem.at[0],
            recv_sem=recv_sem.at[row],
            device_id={"comp": target},
            device_id_type=mesh_id,
        )

    def remote_rest(o, source, target):
        return pltpu.make_async_remote_copy(
            src_ref=rest_send.at[target],
            dst_ref=rest_recv.at[source],
            send_sem=rest_ssem.at[0],
            recv_sem=rest_rsem.at[0],
            device_id={"comp": target},
            device_id_type=mesh_id,
        )

    def sweep(row, count, first_group, last_group):
        size = last_group - first_group

        @pl.loop(0, count * size)
        def _(i):
            start = pl.multiple_of((first_group + lax.rem(i, size)) * PACK, PACK)
            upwind(row + i // size, start, False)

    def scatter(row, count, first, size):
        for o in range(1, n):
            remote(row, count, first, size, o).start()

    def spread_rows(row, count):
        sweep(row, count, 0, main // PACK)
        scatter(row, count, 0, main)
        here = pl.ds(row, count)
        recv[me, here] = send[me, here]

    loaded(0, 0).wait()
    turn_in(0, 0, cut // PACK, False)
    sweep(PAIR, PAIR, 0, cut // PACK)
    pl.semaphore_wait(barrier, devices - 1)
    scatter(PAIR, PAIR, 0, cut)
    loaded(0, 1).wait()
    turn_in(0, cut // PACK, main // PACK, True)
    sweep(PAIR, PAIR, cut // PACK, main // PACK)
    scatter(PAIR, PAIR, cut, main - cut)
    recv[me, PAIR : 2 * PAIR] = send[me, PAIR : 2 * PAIR]
    spread_rows(2 * PAIR, PAIR)
    for h in range(1, halves):
        for p in range(2):
            loaded(h, p).wait()
    last_quarter = rows // QUARTER - 1
    turn_in(last_quarter, 0, main // PACK, True)

    to_below = pltpu.make_async_remote_copy(
        src_ref=xs.at[pl.ds(rows, 1)],
        dst_ref=xs.at[pl.ds(0, 1)],
        send_sem=z_send.at[0],
        recv_sem=z_recv.at[0],
        device_id=below,
        device_id_type=mesh_id,
    )
    to_above = pltpu.make_async_remote_copy(
        src_ref=xs.at[pl.ds(1, 1)],
        dst_ref=xs.at[pl.ds(rows + 1, 1)],
        send_sem=z_send.at[1],
        recv_sem=z_recv.at[1],
        device_id=above,
        device_id_type=mesh_id,
    )

    @pl.when(jnp.logical_not(is_bottom))
    def _():
        to_below.start()

    @pl.when(jnp.logical_not(is_top))
    def _():
        to_above.start()

    turn_in(1, 0, main // PACK, True)
    spread_rows(3 * PAIR, PAIR)
    for c in range(2, last_quarter):
        turn_in(c, 0, main // PACK, True)

    per_quarter = QUARTER // PAIR

    @pl.loop(per_quarter // 2, per_quarter)
    def _(q):
        spread_rows(q * 2 * PAIR, 2 * PAIR)

    @pl.when(jnp.logical_not(is_top))
    def _():
        to_below.wait_recv()

    @pl.when(jnp.logical_not(is_bottom))
    def _():
        to_above.wait_recv()

    if rest:

        @pl.loop(0, rows)
        def _(i):
            upwind(i, main, True)

    if rest:
        rest_send[...] = rest_f[...].astype(BF16)
        for o in range(1, n):
            remote_rest(o, me, lax.rem(me + o, n)).start()
        rest_recv[me] = rest_send[me]

    spread_rows(0, PAIR)

    for i in range(2, len(smalls)):
        small(i).wait()

    lane_d = lax.broadcasted_iota(jnp.int32, (devices, LANES), 0)
    up_to = lax.broadcasted_iota(jnp.int32, (LANES, 2 * LANES), 0)
    at = lax.broadcasted_iota(jnp.int32, (LANES, 2 * LANES), 1)
    counting = jnp.where(jnp.logical_or(up_to < at, at >= LANES), 1.0, 0.0).astype(BF16)
    base[...] = jnp.zeros(base.shape, F32)

    @pl.loop(0, rows)
    def _(r):
        hit = jnp.where(owner[pl.ds(r, 1), :] == lane_d, 1.0, 0.0)
        counts = jnp.dot(hit.astype(BF16), counting, preferred_element_type=F32)
        before = hit * (counts[:, :LANES] + base[...])
        rank[pl.ds(r, 1), :] = jnp.sum(before, axis=0, keepdims=True).astype(jnp.int32)
        base[...] += counts[:, LANES:]

    sub = lax.broadcasted_iota(jnp.int32, (PACK, LANES), 0)
    slot_lane = lax.broadcasted_iota(jnp.int32, (LANES, LANES), 0)
    owner_of = lax.broadcasted_iota(jnp.int32, (devices, PACK, LANES), 0)

    def pack(row, items):
        place = rank[pl.ds(row, 1), :]
        block, lane = place // LANES, lax.rem(place, LANES)
        rows_of = jnp.zeros((PACK, LANES), F32)
        for f in range(len(items)):
            for b in range(nb):
                here = jnp.logical_and(sub == f * nb + b, block == b)
                rows_of = jnp.where(here, items[f], rows_of)
        mine = owner[pl.ds(row, 1), :][None] == owner_of
        spread = jnp.where(mine, rows_of[None], 0.0).astype(BF16)
        onehot = jnp.where(lane == slot_lane, 1.0, 0.0).astype(BF16)
        return spread.reshape(devices * PACK, LANES), onehot

    def pack_rows(row, items):
        halves_of = [pack(row + a, items[a]) for a in range(len(items))]
        packed_acc[...] += nt_dot(
            jnp.concatenate([h[0] for h in halves_of], axis=1),
            jnp.concatenate([h[1] for h in halves_of], axis=1),
        )

    def route(which, comp, at_tile):
        return pltpu.make_async_remote_copy(
            src_ref=packed.at[which, comp * n_tile + at_tile],
            dst_ref=got.at[which, number],
            send_sem=route_ssem.at[which],
            recv_sem=route_rsem.at[which],
            device_id={"comp": comp, "tile": at_tile},
            device_id_type=mesh_id,
        )

    def send_packed(which):
        packed[which] = packed_acc[...].astype(BF16).reshape(devices, PACK, LANES)

        def start(comp, at_tile):
            route(which, comp, at_tile).start()

        others(start)
        got[which, number] = packed[which, number]

    def wait_packed(which):
        all_of(got.at[which, pl.ds(0, devices - 1)], route_rsem.at[which]).wait()

    packed_acc[...] = jnp.zeros(packed_acc.shape, F32)

    @pl.loop(0, steps)
    def _(i):
        items = []
        for a in range(PAIR):
            c = cell[pl.ds(i * PAIR + a, 1), :]
            items.append([(c // cells_c).astype(F32), lax.rem(c, cells_c).astype(F32)])
        pack_rows(i * PAIR, items)

    send_packed(0)
    @pl.loop(per_quarter, per_quarter // 2 * last_quarter)
    def _(q):
        spread_rows(q * 2 * PAIR, 2 * PAIR)

    @pl.loop(per_quarter * last_quarter, steps - 1)
    def _(q):
        spread_rows(q * PAIR, PAIR)

    @pl.loop(rows - PAIR, rows)
    def _(row):
        spread_rows(row, 1)

    to_columns(dissipation, 0)
    to_columns(growth, 1)
    columns[...] = WAVE_STEP * columns[...]

    packed_acc[...] = jnp.zeros(packed_acc.shape, F32)

    get_table.wait()
    bin_high, bin_low = split_two(bins[...].reshape(1, full))
    which = lax.broadcasted_iota(jnp.int32, (PACK, full), 0)
    table[full : full + PACK, :] = jnp.where(
        which == 0, bin_high.astype(F32), jnp.where(which == 1, bin_low.astype(F32), 0.0)
    ).astype(BF16)
    orbit = split_two(orbital[...].reshape(1, full))
    push = split_two(stress[...])
    weight = jnp.zeros((PACK, full), F32)
    for half in range(2):
        lines = [push[half][0:1], push[half][1:2], orbit[half]]
        for f in range(3):
            weight = jnp.where(which == 3 * half + f, lines[f].astype(F32), weight)
    weights[...] = weight.astype(BF16)

    band = 3 * PACK if full % (3 * PACK) == 0 else PACK

    def mix(row, count):
        wide = count * cols
        for s in range(n):
            for a in range(count):
                span = slice(a * cols, (a + 1) * cols)
                whole[s * own : s * own + main, span] = recv[s, row + a].astype(F32)
                if rest:
                    whole[s * own + main : (s + 1) * own, span] = rest_f[
                        s, pl.ds((row + a) * rest, rest), :
                    ]
        acc[:, :wide] = jnp.dot(
            table[...], whole[:, :wide].astype(BF16), preferred_element_type=F32
        )
        total = acc[full : full + 1, :wide] + acc[full + 1 : full + 2, :wide]
        ratio = total / (total + 1.0)
        gust = jnp.concatenate([wind[pl.ds(row + a, 1), :] for a in range(count)], axis=1)
        open_water = jnp.concatenate(
            [wet[pl.ds(row + a, 1), :].astype(F32) for a in range(count)], axis=1
        )
        spot = lax.rem(row, QUARTER)

        @pl.loop(0, full // band)
        def _(b):
            part = pl.ds(pl.multiple_of(b * band, band), band)
            damping, growing = columns[0, part, :], columns[1, part, :]
            for a in range(count):
                span = slice(a * cols, (a + 1) * cols)
                gain = 1.0 - damping * ratio[:, span] + growing * gust[:, span]
                relaxed = WAVE_STEP * acc[part, span] + whole[part, span] * gain
                fresh = open_water[:, span] * jnp.maximum(relaxed, 0.0)
                stage[spot + a, part, :] = fresh.astype(BF16)

        fresh_all = jnp.concatenate([stage[spot + a] for a in range(count)], axis=1)
        pulled = jnp.dot(weights[...], fresh_all, preferred_element_type=F32)
        forces = pulled[0:3] + pulled[3:6]
        pack_rows(
            row,
            [
                [forces[f : f + 1, a * cols : (a + 1) * cols] for f in range(3)]
                for a in range(count)
            ],
        )

    def wait_rows(row, count):
        block = recv.at[pl.ds(0, n - 1), pl.ds(row, count)]
        all_of(block, recv_sem.at[row]).wait()

    def mix_step(q):
        wait_rows(q * PAIR, PAIR)
        mix(q * PAIR, PAIR)

    def turn_out(c):
        @pl.loop(0, full // PACK)
        def _(g):
            part = pl.ds(pl.multiple_of(g * PACK, PACK), PACK)
            block = stage[:, part, :].astype(F32)
            out[part, c * QUARTER : (c + 1) * QUARTER, :] = jnp.swapaxes(block, 0, 1).astype(BF16)

    if rest:
        all_of(rest_recv.at[pl.ds(0, n - 1)], rest_rsem.at[0]).wait()
        rest_f[...] = rest_recv[...].astype(F32)

    @pl.loop(0, per_quarter)
    def _(step):
        mix_step(lax.rem(step + 1, per_quarter))

    turn_out(0)

    for c in range(1, rows // QUARTER):
        if c == last_quarter:
            wait_packed(0)

            @pl.loop(0, devices)
            def _(s):
                cells = got[0, s].astype(F32)
                for b in range(nb):
                    spot = pl.ds(pl.multiple_of((s * nb + b) * LANES, LANES), LANES)
                    col = cells[nb + b : nb + b + 1, :]
                    targets[:, spot] = jnp.where(col == slot_lane.astype(F32), 1.0, 0.0).astype(BF16)

        if c < last_quarter:

            @pl.loop(c * per_quarter // 2, (c + 1) * per_quarter // 2)
            def _(p):
                wait_rows(p * 2 * PAIR, 2 * PAIR)
                for a in range(2):
                    mix((p * 2 + a) * PAIR, PAIR)

        else:

            @pl.loop(c * per_quarter, (c + 1) * per_quarter - 1)
            def _(q):
                mix_step(q)

            @pl.loop(rows - PAIR, rows)
            def _(row):
                wait_rows(row, 1)
                mix(row, 1)

        if c == last_quarter:
            send_packed(1)
        turn_out(c)

    wait_packed(1)
    cell_row = lax.broadcasted_iota(jnp.int32, (cells_r, LANES), 0).astype(F32)

    bottom = jnp.zeros((3 * cells_r, cells_c), F32)
    share = min(devices, SHARE)
    for start in range(0, devices, share):

        @pl.loop(0, share)
        def _(i):
            cells = got[0, start + i].astype(F32)
            force = got[1, start + i].astype(F32)
            for b in range(nb):
                spot = pl.ds(pl.multiple_of((i * nb + b) * LANES, LANES), LANES)
                hit = cells[b : b + 1, :] == cell_row
                for f in range(3):
                    lifted[f * cells_r : (f + 1) * cells_r, spot] = jnp.where(
                        hit, force[f * nb + b : f * nb + b + 1, :], 0.0
                    ).astype(BF16)

        these = slice(start * nb * LANES, (start + share) * nb * LANES)
        bottom += nt_dot(lifted[...], targets[:, these])

    shear_x = current[0] + bottom[0:cells_r]
    shear_y = current[1] + bottom[cells_r : 2 * cells_r]
    shear = jnp.sqrt(shear_x * shear_x + shear_y * shear_y + bottom[2 * cells_r :])
    classes = sediment.shape[0]
    count = classes + metals.shape[0]
    low_share = 0.5 / classes
    high_share = 1.0 - (classes - 1) * low_share
    wetness = roms[...].astype(F32)
    for s in range(classes):
        fraction = jnp.where(bed[...] == s, high_share, low_share)
        rate, critical, settling = [props[i : i + 1, s : s + 1] for i in range(3)]
        erosion = rate * fraction * jnp.maximum(shear / critical - 1.0, 0.0)
        here = sediment[s]
        fields[s] = wetness * (here + SEDIMENT_STEP * (erosion - settling * here))
    for m in range(count - classes):
        fields[classes + m] = wetness * metals[m]

    held = fields[...]
    edge_s[0] = held[:, cells_r - 1, :]
    edge_s[1] = held[:, 0, :]
    turned = held.reshape(count * cells_r, cells_c).T
    edge_s[2, 0:1, :] = turned[cells_c - 1 :]
    edge_s[3, 0:1, :] = turned[0:1]

    def halo(i, device):
        return pltpu.make_async_remote_copy(
            src_ref=edge_s.at[i],
            dst_ref=edge_r.at[i],
            send_sem=halo_ssem.at[i],
            recv_sem=halo_rsem.at[i],
            device_id=device,
            device_id_type=mesh_id,
        )

    halos = [halo(0, below), halo(1, above), halo(2, east_of), halo(3, west_of)]
    sends = [is_bottom, is_top, is_right, is_left]
    receives = [is_top, is_bottom, is_left, is_right]
    for i in range(4):
        pl.when(jnp.logical_not(sends[i]))(halos[i].start)
    for i in range(4):
        pl.when(jnp.logical_not(receives[i]))(halos[i].wait_recv)

    north = jnp.concatenate([edge_r[0][:, None, :], held[:, :-1, :]], axis=1)
    south = jnp.concatenate([held[:, 1:, :], edge_r[1][:, None, :]], axis=1)
    flat = held.reshape(count * cells_r, cells_c)
    lane = lax.broadcasted_iota(jnp.int32, flat.shape, 1)

    def column(i):
        return jnp.broadcast_to(edge_r[i, 0:1, :], (cells_c, count * cells_r)).T

    west = jnp.where(lane == 0, column(2), pltpu.roll(flat, 1, 1)).reshape(held.shape)
    east = jnp.where(lane == cells_c - 1, column(3), pltpu.roll(flat, cells_c - 1, 1)).reshape(
        held.shape
    )
    beside = north + south + west + east
    result[...] = wetness[None] * (held + DIFFUSION * (beside - 4.0 * held))

    for i in range(4):
        pl.when(jnp.logical_not(sends[i]))(halos[i].wait_send)
    pl.when(jnp.logical_not(is_bottom))(to_below.wait_send)
    pl.when(jnp.logical_not(is_top))(to_above.wait_send)

    all_of(send.at[pl.ds(0, n - 1)], send_sem.at[0]).wait()
    if rest:
        all_of(rest_send.at[pl.ds(0, n - 1)], rest_ssem.at[0]).wait()
    for which in range(2):
        all_of(packed.at[which, pl.ds(0, devices - 1)], route_ssem.at[which]).wait()


def finish_kernel(
    fresh,
    diffused,
    partition,
    spectrum_hbm,
    sediment_hbm,
    dissolved_hbm,
    sorbed_hbm,
    dissolved,
    sorbed,
    big_sem,
    field_sem,
):
    full = fresh.shape[0]
    size = -(-full // PIECES)
    spans = [pl.ds(i, min(size, full - i)) for i in range(0, full, size)]
    copies = [
        pltpu.make_async_copy(fresh.at[span], spectrum_hbm.at[span], big_sem.at[i])
        for i, span in enumerate(spans)
    ]
    classes = sediment_hbm.shape[0]
    copies.append(
        pltpu.make_async_copy(diffused.at[pl.ds(0, classes)], sediment_hbm, field_sem.at[0])
    )
    for copy in copies:
        copy.start()
    for m in range(dissolved.shape[0]):
        denominator = 1.0 + sum(
            partition[m : m + 1, s : s + 1] * diffused[s] for s in range(classes)
        )
        spread = diffused[classes + m]
        quotient = spread / denominator
        dissolved[m] = quotient
        sorbed[m] = spread - quotient
    copies.append(pltpu.make_async_copy(dissolved, dissolved_hbm, field_sem.at[1]))
    copies.append(pltpu.make_async_copy(sorbed, sorbed_hbm, field_sem.at[2]))
    for copy in copies[-2:]:
        copy.start()
    for copy in copies:
        copy.wait()


def on_device(
    spectrum,
    courant_x,
    courant_y,
    growth,
    dissipation,
    bin_width,
    transfer,
    stress_weights,
    orbital_weights,
    wind,
    wave_wet,
    owner,
    cell_index,
    current_stress,
    sediment,
    metals,
    bed_class,
    roms_wet,
    class_props,
    partition,
):
    n = lax.axis_size("comp")
    n_tile = lax.axis_size("tile")
    devices = n * n_tile
    own, rows, width = spectrum.shape
    cols = width // n
    full = n * own
    main = own // PACK * PACK
    rest = own - main
    padded = main + (PACK if rest else 0)
    rest_rows = max(rest, 1) * rows
    slots = max(2, 3 * rows * cols // devices)
    nb = -(-slots // LANES)
    steps = rows // PAIR
    classes, cells_r, cells_c = sediment.shape
    count = classes + metals.shape[0]

    operands = (
        spectrum,
        courant_x,
        courant_y,
        growth,
        dissipation,
        bin_width,
        transfer,
        stress_weights,
        orbital_weights,
        wind,
        wave_wet,
        owner.reshape(rows, cols),
        cell_index.reshape(rows, cols),
        current_stress,
        sediment,
        metals,
        bed_class,
        roms_wet,
        class_props,
    )
    vmem = pl.BlockSpec(memory_space=pltpu.VMEM)
    hbm = pl.BlockSpec(memory_space=pltpu.HBM)

    def like(i):
        return pltpu.VMEM(operands[i].shape, operands[i].dtype)

    dma = pltpu.SemaphoreType.DMA
    scratch = [
        *[like(i) for i in range(1, 6)],
        pltpu.VMEM((full + PACK, full), BF16),
        *[like(i) for i in range(7, len(operands))],
        pltpu.VMEM((2, full, LANES), F32),
        pltpu.VMEM((5, padded, cols), F32),
        pltpu.VMEM((rows + 2, padded, width), BF16),
        pltpu.VMEM((n, rows, main, cols), BF16),
        pltpu.VMEM((n, rows, main, cols), BF16),
        pltpu.VMEM((n, rest_rows, cols), F32),
        pltpu.VMEM((n, rest_rows, cols), BF16),
        pltpu.VMEM((n, rest_rows, cols), BF16),
        pltpu.VMEM((full, PAIR * cols), F32),
        pltpu.VMEM((full + PACK, PAIR * cols), F32),
        pltpu.VMEM((QUARTER, full, cols), BF16),
        pltpu.VMEM((PACK, full), BF16),
        pltpu.VMEM((rows, cols), jnp.int32),
        pltpu.VMEM((devices, LANES), F32),
        pltpu.VMEM((devices * PACK, LANES), F32),
        pltpu.VMEM((2, devices, PACK, LANES), BF16),
        pltpu.VMEM((2, devices, PACK, LANES), BF16),
        pltpu.VMEM((LANES, devices * nb * LANES), BF16),
        pltpu.VMEM((3 * cells_r, min(devices, SHARE) * nb * LANES), BF16),
        pltpu.VMEM((count, cells_r, cells_c), F32),
        pltpu.VMEM((4, count, cells_c), F32),
        pltpu.VMEM((4, count, cells_c), F32),
        dma((len(operands) - 2,)),
        dma((rows // PACK, 2)),
        dma((1,)),
        dma((2,)),
        dma((2,)),
        dma((1,)),
        dma((rows,)),
        dma((1,)),
        dma((1,)),
        dma((2,)),
        dma((2,)),
        dma((4,)),
        dma((4,)),
    ]
    fresh, diffused = pl.pallas_call(
        functools.partial(step_kernel, n, n_tile, slots),
        out_shape=(
            pltpu.VMEM((full, rows, cols), BF16),
            pltpu.VMEM((count, cells_r, cells_c), F32),
        ),
        in_specs=[hbm] * len(operands),
        out_specs=(vmem, vmem),
        scratch_shapes=scratch,
        compiler_params=pltpu.CompilerParams(
            collective_id=0, has_side_effects=True, vmem_limit_bytes=54000 * 1024
        ),
    )(*operands)

    field = jax.ShapeDtypeStruct((classes, cells_r, cells_c), F32)
    metal = jax.ShapeDtypeStruct((count - classes, cells_r, cells_c), F32)
    return tuple(
        pl.pallas_call(
            finish_kernel,
            out_shape=(jax.ShapeDtypeStruct(fresh.shape, fresh.dtype), field, metal, metal),
            in_specs=[pl.BlockSpec(memory_space=pl.ANY), vmem, vmem],
            out_specs=(hbm,) * 4,
            scratch_shapes=[
                pltpu.VMEM(metal.shape, F32),
                pltpu.VMEM(metal.shape, F32),
                dma((PIECES,)),
                dma((3,)),
            ],
            compiler_params=pltpu.CompilerParams(vmem_limit_bytes=4 << 20),
        )(
            pltpu.with_memory_space_constraint(fresh, pltpu.VMEM),
            pltpu.with_memory_space_constraint(diffused, pltpu.VMEM),
            partition,
        )
    )


def solution(mesh):
    replicated = P()
    grid = P("tile", "comp")
    fields = P(None, "tile", "comp")
    in_specs = (
        P("comp", "tile", None),
        *[replicated] * 8,
        grid,
        grid,
        P("tile", "comp", None, None, None),
        P("tile", "comp", None, None),
        fields,
        fields,
        fields,
        grid,
        grid,
        replicated,
        replicated,
    )
    return jax.shard_map(
        on_device, mesh=mesh, in_specs=in_specs, out_specs=(fields,) * 4, check_vma=False
    )
```

```python
import functools

import jax
import jax.numpy as jnp
from jax import lax
from jax.experimental import pallas as pl
from jax.experimental.pallas import tpu as pltpu
from jax.sharding import PartitionSpec as P

WAVE_STEP = 0.5
SEDIMENT_STEP = 1.0
DIFFUSION = 0.2
LANES = 128
PACK = 16
PAIR = 2
QUARTER = 8
SHARE = 32
PARTS = 3
PIECES = 8
F32 = jnp.float32
BF16 = jnp.bfloat16


def nt_dot(a, b):
    return lax.dot_general(a, b, (((1,), (1,)), ((), ())), preferred_element_type=F32)


def split_two(values):
    high = values.astype(BF16)
    return high, (values - high.astype(F32)).astype(BF16)


def step_kernel(
    n,
    n_tile,
    slots,
    x_hbm,
    cx_hbm,
    cy_hbm,
    grow_hbm,
    damp_hbm,
    bin_hbm,
    transfer_hbm,
    stress_hbm,
    orbital_hbm,
    wind_hbm,
    wet_hbm,
    owner_hbm,
    cell_hbm,
    current_hbm,
    sediment_hbm,
    metals_hbm,
    bed_hbm,
    roms_hbm,
    props_hbm,
    out,
    result,
    cx,
    cy,
    growth,
    dissipation,
    bins,
    table,
    stress,
    orbital,
    wind,
    wet,
    owner,
    cell,
    current,
    sediment,
    metals,
    bed,
    roms,
    props,
    columns,
    coef,
    xs,
    send,
    recv,
    rest_f,
    rest_send,
    rest_recv,
    whole,
    acc,
    stage,
    weights,
    rank,
    base,
    packed_acc,
    packed,
    got,
    cells_s,
    cells_g,
    targets,
    lifted,
    fields,
    edge_s,
    edge_r,
    small_sem,
    in_sem,
    table_sem,
    z_send,
    z_recv,
    send_sem,
    recv_sem,
    rest_ssem,
    rest_rsem,
    route_ssem,
    route_rsem,
    halo_ssem,
    halo_rsem,
):
    me = lax.axis_index("comp")
    tile = lax.axis_index("tile")
    devices = n * n_tile
    number = me * n_tile + tile
    own, rows, width = x_hbm.shape
    cols = width // n
    full = n * own
    main = own // PACK * PACK
    rest = own - main
    groups = main // PACK + (1 if rest else 0)
    steps = rows // PAIR
    halves = rows // PACK
    nb = -(-slots // LANES)
    cells_r, cells_c = result.shape[1], result.shape[2]
    is_top, is_bottom = tile == 0, tile == n_tile - 1
    is_left, is_right = me == 0, me == n - 1
    mesh_id = pl.DeviceIdType.MESH
    above = {"tile": lax.rem(tile + n_tile - 1, n_tile)}
    below = {"tile": lax.rem(tile + 1, n_tile)}
    west_of = {"comp": lax.rem(me + n - 1, n)}
    east_of = {"comp": lax.rem(me + 1, n)}

    def others(act):
        @pl.loop(0, n)
        def _(c):
            comp = lax.rem(me + c, n)
            for t in range(n_tile):
                if t:
                    act(comp, lax.rem(tile + t, n_tile))
                else:
                    pl.when(c > 0)(functools.partial(act, comp, tile))

    smalls = [
        (cx_hbm, cx),
        (cy_hbm, cy),
        (bin_hbm, bins),
        (stress_hbm, stress),
        (orbital_hbm, orbital),
        (grow_hbm, growth),
        (damp_hbm, dissipation),
        (wind_hbm, wind),
        (wet_hbm, wet),
        (owner_hbm, owner),
        (cell_hbm, cell),
        (current_hbm, current),
        (sediment_hbm, sediment),
        (metals_hbm, metals),
        (bed_hbm, bed),
        (roms_hbm, roms),
        (props_hbm, props),
    ]

    def small(i):
        return pltpu.make_async_copy(smalls[i][0], smalls[i][1], small_sem.at[i])

    cuts = [main // PACK * i // PARTS for i in range(PARTS + 1)]
    ends = [c * PACK for c in cuts[:-1]] + [own]
    parts = [(ends[p], ends[p + 1] - ends[p]) for p in range(PARTS)]

    def load(h, p, d):
        first, size = parts[p]
        return pltpu.make_async_copy(
            x_hbm.at[pl.ds(first, size), pl.ds(h * PACK, PACK), pl.ds(d * cols, cols)],
            out.at[pl.ds(d * own + first, size), pl.ds(h * PACK, PACK), :],
            in_sem.at[h, p],
        )

    def loaded(h, p):
        block = out.at[pl.ds(0, n * parts[p][1]), pl.ds(h * PACK, PACK), :]
        return pltpu.make_async_copy(block, block, in_sem.at[h, p])

    def all_of(block, sem):
        return pltpu.make_async_copy(block, block, sem)

    small(0).start()
    small(1).start()
    for p in range(PARTS):
        for d in range(n):
            load(0, p, d).start()

    barrier = pltpu.get_barrier_semaphore()

    def greet(comp, at_tile):
        pl.semaphore_signal(
            barrier, inc=1, device_id={"comp": comp, "tile": at_tile}, device_id_type=mesh_id
        )

    others(greet)
    for h in range(1, halves):
        for p in range(PARTS):
            for d in range(n):
                load(h, p, d).start()
    for i in range(2, len(smalls)):
        small(i).start()
    get_table = pltpu.make_async_copy(transfer_hbm, table.at[pl.ds(0, full)], table_sem.at[0])
    get_table.start()

    def to_columns(values, i):
        for b in range(0, full, LANES):
            size = min(LANES, full - b)
            line = values[pl.ds(b, size)].reshape(1, size)
            columns[i, b : b + size, :] = jnp.broadcast_to(line, (LANES, size)).T

    small(0).wait()
    small(1).wait()
    to_columns(cx, 0)
    to_columns(cy, 1)

    for g in range(groups):
        first = g * PACK if g * PACK < main else own - PACK
        speed_x = columns[0, pl.ds(me * own + first, PACK), :]
        speed_y = columns[1, pl.ds(me * own + first, PACK), :]
        part = slice(g * PACK, (g + 1) * PACK)
        coef[0, part, :] = 1.0 - jnp.abs(speed_x) - jnp.abs(speed_y)
        coef[1, part, :] = jnp.maximum(speed_x, 0.0)
        coef[2, part, :] = -jnp.minimum(speed_x, 0.0)
        coef[3, part, :] = jnp.maximum(speed_y, 0.0)
        coef[4, part, :] = -jnp.minimum(speed_y, 0.0)

    @pl.when(is_top)
    def _():
        xs[0] = jnp.zeros(xs.shape[1:], BF16)
        edge_r[0] = jnp.zeros(edge_r.shape[1:], F32)

    @pl.when(is_bottom)
    def _():
        xs[rows + 1] = jnp.zeros(xs.shape[1:], BF16)
        edge_r[1] = jnp.zeros(edge_r.shape[1:], F32)

    @pl.when(is_left)
    def _():
        edge_r[2] = jnp.zeros(edge_r.shape[1:], F32)

    @pl.when(is_right)
    def _():
        edge_r[3] = jnp.zeros(edge_r.shape[1:], F32)

    def turn_in(c, first_group, last_group, with_rest):
        top = c * QUARTER
        for d in range(n):

            def piece(at, first):
                block = out[pl.ds(d * own + first, PACK), top : top + QUARTER, :].astype(F32)
                xs[1 + top : 1 + top + QUARTER, pl.ds(at, PACK), d * cols : (d + 1) * cols] = (
                    jnp.swapaxes(block, 0, 1).astype(BF16)
                )

            @pl.loop(first_group, last_group)
            def _(g):
                start = pl.multiple_of(g * PACK, PACK)
                piece(start, start)

            if rest and with_rest:
                piece(main, own - PACK)

    def upwind(row, start, is_rest):
        part = pl.ds(start, PACK)
        lane = lax.broadcasted_iota(jnp.int32, (PACK, cols), 1)
        first_lane, last_lane = lane == 0, lane == cols - 1
        kept, from_north, from_south, from_west, from_east = [coef[i, part, :] for i in range(5)]

        def tile_of(at, d):
            return xs[at, part, d * cols : (d + 1) * cols].astype(F32)

        centre = [tile_of(row + 1, d) for d in range(n)]
        right = [pltpu.roll(c, 1, 1) for c in centre]
        left = [pltpu.roll(c, cols - 1, 1) for c in centre]
        nothing = jnp.zeros((PACK, cols), F32)
        for d in range(n):
            west = jnp.where(first_lane, right[d - 1] if d else nothing, right[d])
            east = jnp.where(last_lane, left[d + 1] if d < n - 1 else nothing, left[d])
            moved = (
                kept * centre[d]
                + from_north * tile_of(row, d)
                + from_south * tile_of(row + 2, d)
                + from_west * west
                + from_east * east
            )
            if is_rest:
                rest_f[d, pl.ds(row * rest, rest), :] = moved[PACK - rest :]
            else:
                send[d, row, part, :] = moved.astype(BF16)

    def remote(row, count, first, size, o):
        here = pl.ds(row, count), pl.ds(first, size)
        target = lax.rem(me + o, n)
        return pltpu.make_async_remote_copy(
            src_ref=send.at[target, *here],
            dst_ref=recv.at[me, *here],
            send_sem=send_sem.at[0],
            recv_sem=recv_sem.at[row],
            device_id={"comp": target},
            device_id_type=mesh_id,
        )

    def remote_rest(o, source, target):
        return pltpu.make_async_remote_copy(
            src_ref=rest_send.at[target],
            dst_ref=rest_recv.at[source],
            send_sem=rest_ssem.at[0],
            recv_sem=rest_rsem.at[0],
            device_id={"comp": target},
            device_id_type=mesh_id,
        )

    def sweep(row, count, first_group, last_group):
        size = last_group - first_group

        @pl.loop(0, count * size)
        def _(i):
            start = pl.multiple_of((first_group + lax.rem(i, size)) * PACK, PACK)
            upwind(row + i // size, start, False)

    def scatter(row, count, first, size):
        for o in range(1, n):
            remote(row, count, first, size, o).start()

    def spread_rows(row, count):
        sweep(row, count, 0, main // PACK)
        scatter(row, count, 0, main)
        here = pl.ds(row, count)
        recv[me, here] = send[me, here]

    for p in range(PARTS):
        loaded(0, p).wait()
        turn_in(0, cuts[p], cuts[p + 1], p == PARTS - 1)
        sweep(PAIR, PAIR, cuts[p], cuts[p + 1])
        if p == 0:
            pl.semaphore_wait(barrier, devices - 1)
        scatter(PAIR, PAIR, cuts[p] * PACK, (cuts[p + 1] - cuts[p]) * PACK)
    recv[me, PAIR : 2 * PAIR] = send[me, PAIR : 2 * PAIR]
    spread_rows(2 * PAIR, PAIR)
    for h in range(1, halves):
        for p in range(PARTS):
            loaded(h, p).wait()
    last_quarter = rows // QUARTER - 1
    turn_in(last_quarter, 0, main // PACK, True)

    to_below = pltpu.make_async_remote_copy(
        src_ref=xs.at[pl.ds(rows, 1)],
        dst_ref=xs.at[pl.ds(0, 1)],
        send_sem=z_send.at[0],
        recv_sem=z_recv.at[0],
        device_id=below,
        device_id_type=mesh_id,
    )
    to_above = pltpu.make_async_remote_copy(
        src_ref=xs.at[pl.ds(1, 1)],
        dst_ref=xs.at[pl.ds(rows + 1, 1)],
        send_sem=z_send.at[1],
        recv_sem=z_recv.at[1],
        device_id=above,
        device_id_type=mesh_id,
    )

    @pl.when(jnp.logical_not(is_bottom))
    def _():
        to_below.start()

    @pl.when(jnp.logical_not(is_top))
    def _():
        to_above.start()

    turn_in(1, 0, main // PACK, True)
    spread_rows(3 * PAIR, PAIR)
    for c in range(2, last_quarter):
        turn_in(c, 0, main // PACK, True)

    per_quarter = QUARTER // PAIR

    spread_rows(QUARTER, QUARTER)

    @pl.when(jnp.logical_not(is_top))
    def _():
        to_below.wait_recv()

    @pl.when(jnp.logical_not(is_bottom))
    def _():
        to_above.wait_recv()

    if rest:

        @pl.loop(0, rows)
        def _(i):
            upwind(i, main, True)

    if rest:
        rest_send[...] = rest_f[...].astype(BF16)
        for o in range(1, n):
            remote_rest(o, me, lax.rem(me + o, n)).start()
        rest_recv[me] = rest_send[me]

    spread_rows(0, PAIR)

    for i in range(2, len(smalls)):
        small(i).wait()

    lane_d = lax.broadcasted_iota(jnp.int32, (devices, LANES), 0)
    up_to = lax.broadcasted_iota(jnp.int32, (LANES, 2 * LANES), 0)
    at = lax.broadcasted_iota(jnp.int32, (LANES, 2 * LANES), 1)
    counting = jnp.where(jnp.logical_or(up_to < at, at >= LANES), 1.0, 0.0).astype(BF16)
    base[...] = jnp.zeros(base.shape, F32)

    @pl.loop(0, rows)
    def _(r):
        hit = jnp.where(owner[pl.ds(r, 1), :] == lane_d, 1.0, 0.0)
        counts = jnp.dot(hit.astype(BF16), counting, preferred_element_type=F32)
        before = hit * (counts[:, :LANES] + base[...])
        rank[pl.ds(r, 1), :] = jnp.sum(before, axis=0, keepdims=True).astype(jnp.int32)
        base[...] += counts[:, LANES:]

    sub = lax.broadcasted_iota(jnp.int32, (PACK, LANES), 0)
    slot_lane = lax.broadcasted_iota(jnp.int32, (LANES, LANES), 0)
    owner_of = lax.broadcasted_iota(jnp.int32, (devices, PACK, LANES), 0)

    def pack(row, items):
        place = rank[pl.ds(row, 1), :]
        block, lane = place // LANES, lax.rem(place, LANES)
        rows_of = jnp.zeros((PACK, LANES), F32)
        for f in range(len(items)):
            for b in range(nb):
                here = jnp.logical_and(sub == f * nb + b, block == b)
                rows_of = jnp.where(here, items[f], rows_of)
        mine = owner[pl.ds(row, 1), :][None] == owner_of
        spread = jnp.where(mine, rows_of[None], 0.0).astype(BF16)
        onehot = jnp.where(lane == slot_lane, 1.0, 0.0).astype(BF16)
        return spread.reshape(devices * PACK, LANES), onehot

    def pack_rows(row, items):
        halves_of = [pack(row + a, items[a]) for a in range(len(items))]
        packed_acc[...] += nt_dot(
            jnp.concatenate([h[0] for h in halves_of], axis=1),
            jnp.concatenate([h[1] for h in halves_of], axis=1),
        )

    routes = [(cells_s, cells_g), (packed, got)]

    def send_packed(which):
        source, target = routes[which]
        count = source.shape[1]
        block = packed_acc[...].astype(BF16).reshape(devices, PACK, LANES)
        source[...] = block[:, :count, :]

        def start(comp, at_tile):
            pltpu.make_async_remote_copy(
                src_ref=source.at[comp * n_tile + at_tile],
                dst_ref=target.at[number],
                send_sem=route_ssem.at[which],
                recv_sem=route_rsem.at[which],
                device_id={"comp": comp, "tile": at_tile},
                device_id_type=mesh_id,
            ).start()

        others(start)
        target[number] = source[number]

    def wait_packed(which):
        block = routes[which][1].at[pl.ds(0, devices - 1)]
        all_of(block, route_rsem.at[which]).wait()

    packed_acc[...] = jnp.zeros(packed_acc.shape, F32)

    @pl.loop(0, steps)
    def _(i):
        items = []
        for a in range(PAIR):
            c = cell[pl.ds(i * PAIR + a, 1), :]
            items.append([(c // cells_c).astype(F32), lax.rem(c, cells_c).astype(F32)])
        pack_rows(i * PAIR, items)

    send_packed(0)
    @pl.loop(2, last_quarter)
    def _(c):
        spread_rows(c * QUARTER, QUARTER)

    @pl.loop(per_quarter * last_quarter, steps - 1)
    def _(q):
        spread_rows(q * PAIR, PAIR)

    @pl.loop(rows - PAIR, rows)
    def _(row):
        spread_rows(row, 1)

    to_columns(dissipation, 0)
    to_columns(growth, 1)
    columns[...] = WAVE_STEP * columns[...]

    packed_acc[...] = jnp.zeros(packed_acc.shape, F32)

    get_table.wait()
    bin_high, bin_low = split_two(bins[...].reshape(1, full))
    which = lax.broadcasted_iota(jnp.int32, (PACK, full), 0)
    table[full : full + PACK, :] = jnp.where(
        which == 0, bin_high.astype(F32), jnp.where(which == 1, bin_low.astype(F32), 0.0)
    ).astype(BF16)
    orbit = split_two(orbital[...].reshape(1, full))
    push = split_two(stress[...])
    weight = jnp.zeros((PACK, full), F32)
    for half in range(2):
        lines = [push[half][0:1], push[half][1:2], orbit[half]]
        for f in range(3):
            weight = jnp.where(which == 3 * half + f, lines[f].astype(F32), weight)
    weights[...] = weight.astype(BF16)

    band = 3 * PACK if full % (3 * PACK) == 0 else PACK

    def mix(row, count):
        wide = count * cols
        for s in range(n):
            for a in range(count):
                span = slice(a * cols, (a + 1) * cols)
                whole[s * own : s * own + main, span] = recv[s, row + a].astype(F32)
                if rest:
                    whole[s * own + main : (s + 1) * own, span] = rest_f[
                        s, pl.ds((row + a) * rest, rest), :
                    ]
        acc[:, :wide] = jnp.dot(
            table[...], whole[:, :wide].astype(BF16), preferred_element_type=F32
        )
        total = acc[full : full + 1, :wide] + acc[full + 1 : full + 2, :wide]
        ratio = total / (total + 1.0)
        gust = jnp.concatenate([wind[pl.ds(row + a, 1), :] for a in range(count)], axis=1)
        open_water = jnp.concatenate(
            [wet[pl.ds(row + a, 1), :].astype(F32) for a in range(count)], axis=1
        )
        spot = lax.rem(row, QUARTER)

        @pl.loop(0, full // band)
        def _(b):
            part = pl.ds(pl.multiple_of(b * band, band), band)
            damping, growing = columns[0, part, :], columns[1, part, :]
            for a in range(count):
                span = slice(a * cols, (a + 1) * cols)
                gain = 1.0 - damping * ratio[:, span] + growing * gust[:, span]
                relaxed = WAVE_STEP * acc[part, span] + whole[part, span] * gain
                fresh = open_water[:, span] * jnp.maximum(relaxed, 0.0)
                stage[spot + a, part, :] = fresh.astype(BF16)

        fresh_all = jnp.concatenate([stage[spot + a] for a in range(count)], axis=1)
        pulled = jnp.dot(weights[...], fresh_all, preferred_element_type=F32)
        forces = pulled[0:3] + pulled[3:6]
        pack_rows(
            row,
            [
                [forces[f : f + 1, a * cols : (a + 1) * cols] for f in range(3)]
                for a in range(count)
            ],
        )

    def wait_rows(row, count):
        block = recv.at[pl.ds(0, n - 1), pl.ds(row, count)]
        all_of(block, recv_sem.at[row]).wait()

    def mix_step(q):
        wait_rows(q * PAIR, PAIR)
        mix(q * PAIR, PAIR)

    def turn_out(c):
        @pl.loop(0, full // PACK)
        def _(g):
            part = pl.ds(pl.multiple_of(g * PACK, PACK), PACK)
            block = stage[:, part, :].astype(F32)
            out[part, c * QUARTER : (c + 1) * QUARTER, :] = jnp.swapaxes(block, 0, 1).astype(BF16)

    if rest:
        all_of(rest_recv.at[pl.ds(0, n - 1)], rest_rsem.at[0]).wait()
        rest_f[...] = rest_recv[...].astype(F32)

    @pl.loop(0, per_quarter)
    def _(step):
        mix_step(lax.rem(step + 1, per_quarter))

    turn_out(0)

    for c in range(1, rows // QUARTER):
        if c == last_quarter:
            wait_packed(0)

            @pl.loop(0, devices)
            def _(s):
                cells = cells_g[s].astype(F32)
                for b in range(nb):
                    spot = pl.ds(pl.multiple_of((s * nb + b) * LANES, LANES), LANES)
                    col = cells[nb + b : nb + b + 1, :]
                    targets[:, spot] = jnp.where(col == slot_lane.astype(F32), 1.0, 0.0).astype(BF16)

        if c < last_quarter:

            wait_rows(c * QUARTER, QUARTER)

            @pl.loop(c * per_quarter, (c + 1) * per_quarter)
            def _(q):
                mix(q * PAIR, PAIR)

        else:

            @pl.loop(c * per_quarter, (c + 1) * per_quarter - 1)
            def _(q):
                mix_step(q)

            @pl.loop(rows - PAIR, rows)
            def _(row):
                wait_rows(row, 1)
                mix(row, 1)

        if c == last_quarter:
            send_packed(1)
        turn_out(c)

    wait_packed(1)
    cell_row = lax.broadcasted_iota(jnp.int32, (cells_r, LANES), 0).astype(F32)

    bottom = jnp.zeros((3 * cells_r, cells_c), F32)
    share = min(devices, SHARE)
    for start in range(0, devices, share):

        @pl.loop(0, share)
        def _(i):
            cells = cells_g[start + i].astype(F32)
            force = got[start + i].astype(F32)
            for b in range(nb):
                spot = pl.ds(pl.multiple_of((i * nb + b) * LANES, LANES), LANES)
                hit = cells[b : b + 1, :] == cell_row
                for f in range(3):
                    lifted[f * cells_r : (f + 1) * cells_r, spot] = jnp.where(
                        hit, force[f * nb + b : f * nb + b + 1, :], 0.0
                    ).astype(BF16)

        these = slice(start * nb * LANES, (start + share) * nb * LANES)
        bottom += nt_dot(lifted[...], targets[:, these])

    shear_x = current[0] + bottom[0:cells_r]
    shear_y = current[1] + bottom[cells_r : 2 * cells_r]
    shear = jnp.sqrt(shear_x * shear_x + shear_y * shear_y + bottom[2 * cells_r :])
    classes = sediment.shape[0]
    count = classes + metals.shape[0]
    low_share = 0.5 / classes
    high_share = 1.0 - (classes - 1) * low_share
    wetness = roms[...].astype(F32)
    for s in range(classes):
        fraction = jnp.where(bed[...] == s, high_share, low_share)
        rate, critical, settling = [props[i : i + 1, s : s + 1] for i in range(3)]
        erosion = rate * fraction * jnp.maximum(shear / critical - 1.0, 0.0)
        here = sediment[s]
        fields[s] = wetness * (here + SEDIMENT_STEP * (erosion - settling * here))
    for m in range(count - classes):
        fields[classes + m] = wetness * metals[m]

    held = fields[...]
    edge_s[0] = held[:, cells_r - 1, :]
    edge_s[1] = held[:, 0, :]
    turned = held.reshape(count * cells_r, cells_c).T
    edge_s[2, 0:1, :] = turned[cells_c - 1 :]
    edge_s[3, 0:1, :] = turned[0:1]

    def halo(i, device):
        return pltpu.make_async_remote_copy(
            src_ref=edge_s.at[i],
            dst_ref=edge_r.at[i],
            send_sem=halo_ssem.at[i],
            recv_sem=halo_rsem.at[i],
            device_id=device,
            device_id_type=mesh_id,
        )

    halos = [halo(0, below), halo(1, above), halo(2, east_of), halo(3, west_of)]
    sends = [is_bottom, is_top, is_right, is_left]
    receives = [is_top, is_bottom, is_left, is_right]
    for i in range(4):
        pl.when(jnp.logical_not(sends[i]))(halos[i].start)
    for i in range(4):
        pl.when(jnp.logical_not(receives[i]))(halos[i].wait_recv)

    north = jnp.concatenate([edge_r[0][:, None, :], held[:, :-1, :]], axis=1)
    south = jnp.concatenate([held[:, 1:, :], edge_r[1][:, None, :]], axis=1)
    flat = held.reshape(count * cells_r, cells_c)
    lane = lax.broadcasted_iota(jnp.int32, flat.shape, 1)

    def column(i):
        return jnp.broadcast_to(edge_r[i, 0:1, :], (cells_c, count * cells_r)).T

    west = jnp.where(lane == 0, column(2), pltpu.roll(flat, 1, 1)).reshape(held.shape)
    east = jnp.where(lane == cells_c - 1, column(3), pltpu.roll(flat, cells_c - 1, 1)).reshape(
        held.shape
    )
    beside = north + south + west + east
    result[...] = wetness[None] * (held + DIFFUSION * (beside - 4.0 * held))

    for i in range(4):
        pl.when(jnp.logical_not(sends[i]))(halos[i].wait_send)
    pl.when(jnp.logical_not(is_bottom))(to_below.wait_send)
    pl.when(jnp.logical_not(is_top))(to_above.wait_send)

    all_of(send.at[pl.ds(0, n - 1)], send_sem.at[0]).wait()
    if rest:
        all_of(rest_send.at[pl.ds(0, n - 1)], rest_ssem.at[0]).wait()
    for which in range(2):
        block = routes[which][0].at[pl.ds(0, devices - 1)]
        all_of(block, route_ssem.at[which]).wait()


def finish_kernel(
    fresh,
    diffused,
    partition,
    spectrum_hbm,
    sediment_hbm,
    dissolved_hbm,
    sorbed_hbm,
    dissolved,
    sorbed,
    big_sem,
    field_sem,
):
    full = fresh.shape[0]
    size = -(-full // PIECES)
    spans = [pl.ds(i, min(size, full - i)) for i in range(0, full, size)]
    copies = [
        pltpu.make_async_copy(fresh.at[span], spectrum_hbm.at[span], big_sem.at[i])
        for i, span in enumerate(spans)
    ]
    classes = sediment_hbm.shape[0]
    copies.append(
        pltpu.make_async_copy(diffused.at[pl.ds(0, classes)], sediment_hbm, field_sem.at[0])
    )
    for copy in copies:
        copy.start()
    for m in range(dissolved.shape[0]):
        denominator = 1.0 + sum(
            partition[m : m + 1, s : s + 1] * diffused[s] for s in range(classes)
        )
        spread = diffused[classes + m]
        quotient = spread / denominator
        dissolved[m] = quotient
        sorbed[m] = spread - quotient
    copies.append(pltpu.make_async_copy(dissolved, dissolved_hbm, field_sem.at[1]))
    copies.append(pltpu.make_async_copy(sorbed, sorbed_hbm, field_sem.at[2]))
    for copy in copies[-2:]:
        copy.start()
    for copy in copies:
        copy.wait()


def on_device(
    spectrum,
    courant_x,
    courant_y,
    growth,
    dissipation,
    bin_width,
    transfer,
    stress_weights,
    orbital_weights,
    wind,
    wave_wet,
    owner,
    cell_index,
    current_stress,
    sediment,
    metals,
    bed_class,
    roms_wet,
    class_props,
    partition,
):
    n = lax.axis_size("comp")
    n_tile = lax.axis_size("tile")
    devices = n * n_tile
    own, rows, width = spectrum.shape
    cols = width // n
    full = n * own
    main = own // PACK * PACK
    rest = own - main
    padded = main + (PACK if rest else 0)
    rest_rows = max(rest, 1) * rows
    slots = max(2, 3 * rows * cols // devices)
    nb = -(-slots // LANES)
    steps = rows // PAIR
    classes, cells_r, cells_c = sediment.shape
    count = classes + metals.shape[0]

    operands = (
        spectrum,
        courant_x,
        courant_y,
        growth,
        dissipation,
        bin_width,
        transfer,
        stress_weights,
        orbital_weights,
        wind,
        wave_wet,
        owner.reshape(rows, cols),
        cell_index.reshape(rows, cols),
        current_stress,
        sediment,
        metals,
        bed_class,
        roms_wet,
        class_props,
    )
    vmem = pl.BlockSpec(memory_space=pltpu.VMEM)
    hbm = pl.BlockSpec(memory_space=pltpu.HBM)

    def like(i):
        return pltpu.VMEM(operands[i].shape, operands[i].dtype)

    dma = pltpu.SemaphoreType.DMA
    scratch = [
        *[like(i) for i in range(1, 6)],
        pltpu.VMEM((full + PACK, full), BF16),
        *[like(i) for i in range(7, len(operands))],
        pltpu.VMEM((2, full, LANES), F32),
        pltpu.VMEM((5, padded, cols), F32),
        pltpu.VMEM((rows + 2, padded, width), BF16),
        pltpu.VMEM((n, rows, main, cols), BF16),
        pltpu.VMEM((n, rows, main, cols), BF16),
        pltpu.VMEM((n, rest_rows, cols), F32),
        pltpu.VMEM((n, rest_rows, cols), BF16),
        pltpu.VMEM((n, rest_rows, cols), BF16),
        pltpu.VMEM((full, PAIR * cols), F32),
        pltpu.VMEM((full + PACK, PAIR * cols), F32),
        pltpu.VMEM((QUARTER, full, cols), BF16),
        pltpu.VMEM((PACK, full), BF16),
        pltpu.VMEM((rows, cols), jnp.int32),
        pltpu.VMEM((devices, LANES), F32),
        pltpu.VMEM((devices * PACK, LANES), F32),
        pltpu.VMEM((devices, PACK, LANES), BF16),
        pltpu.VMEM((devices, PACK, LANES), BF16),
        pltpu.VMEM((devices, 2 * nb, LANES), BF16),
        pltpu.VMEM((devices, 2 * nb, LANES), BF16),
        pltpu.VMEM((LANES, devices * nb * LANES), BF16),
        pltpu.VMEM((3 * cells_r, min(devices, SHARE) * nb * LANES), BF16),
        pltpu.VMEM((count, cells_r, cells_c), F32),
        pltpu.VMEM((4, count, cells_c), F32),
        pltpu.VMEM((4, count, cells_c), F32),
        dma((len(operands) - 2,)),
        dma((rows // PACK, PARTS)),
        dma((1,)),
        dma((2,)),
        dma((2,)),
        dma((1,)),
        dma((rows,)),
        dma((1,)),
        dma((1,)),
        dma((2,)),
        dma((2,)),
        dma((4,)),
        dma((4,)),
    ]
    fresh, diffused = pl.pallas_call(
        functools.partial(step_kernel, n, n_tile, slots),
        out_shape=(
            pltpu.VMEM((full, rows, cols), BF16),
            pltpu.VMEM((count, cells_r, cells_c), F32),
        ),
        in_specs=[hbm] * len(operands),
        out_specs=(vmem, vmem),
        scratch_shapes=scratch,
        compiler_params=pltpu.CompilerParams(
            collective_id=0, has_side_effects=True, vmem_limit_bytes=54000 * 1024
        ),
    )(*operands)

    field = jax.ShapeDtypeStruct((classes, cells_r, cells_c), F32)
    metal = jax.ShapeDtypeStruct((count - classes, cells_r, cells_c), F32)
    return tuple(
        pl.pallas_call(
            finish_kernel,
            out_shape=(jax.ShapeDtypeStruct(fresh.shape, fresh.dtype), field, metal, metal),
            in_specs=[pl.BlockSpec(memory_space=pl.ANY), vmem, vmem],
            out_specs=(hbm,) * 4,
            scratch_shapes=[
                pltpu.VMEM(metal.shape, F32),
                pltpu.VMEM(metal.shape, F32),
                dma((PIECES,)),
                dma((3,)),
            ],
            compiler_params=pltpu.CompilerParams(vmem_limit_bytes=4 << 20),
        )(
            pltpu.with_memory_space_constraint(fresh, pltpu.VMEM),
            pltpu.with_memory_space_constraint(diffused, pltpu.VMEM),
            partition,
        )
    )


def solution(mesh):
    replicated = P()
    grid = P("tile", "comp")
    fields = P(None, "tile", "comp")
    in_specs = (
        P("comp", "tile", None),
        *[replicated] * 8,
        grid,
        grid,
        P("tile", "comp", None, None, None),
        P("tile", "comp", None, None),
        fields,
        fields,
        fields,
        grid,
        grid,
        replicated,
        replicated,
    )
    return jax.shard_map(
        on_device, mesh=mesh, in_specs=in_specs, out_specs=(fields,) * 4, check_vma=False
    )
```

```python
import functools

import jax
import jax.numpy as jnp
from jax import lax
from jax.experimental import pallas as pl
from jax.experimental.pallas import tpu as pltpu
from jax.sharding import PartitionSpec as P

WAVE_STEP = 0.5
SEDIMENT_STEP = 1.0
DIFFUSION = 0.2
LANES = 128
PACK = 16
PAIR = 2
QUARTER = 8
SHARE = 32
PARTS = 3
PIECES = 8
F32 = jnp.float32
BF16 = jnp.bfloat16


def nt_dot(a, b):
    return lax.dot_general(a, b, (((1,), (1,)), ((), ())), preferred_element_type=F32)


def split_two(values):
    high = values.astype(BF16)
    return high, (values - high.astype(F32)).astype(BF16)


def step_kernel(
    n,
    n_tile,
    slots,
    x_hbm,
    cx_hbm,
    cy_hbm,
    grow_hbm,
    damp_hbm,
    bin_hbm,
    transfer_hbm,
    stress_hbm,
    orbital_hbm,
    wind_hbm,
    wet_hbm,
    owner_hbm,
    cell_hbm,
    current_hbm,
    sediment_hbm,
    metals_hbm,
    bed_hbm,
    roms_hbm,
    props_hbm,
    out,
    result,
    cx,
    cy,
    growth,
    dissipation,
    bins,
    table,
    stress,
    orbital,
    wind,
    wet,
    owner,
    cell,
    current,
    sediment,
    metals,
    bed,
    roms,
    props,
    columns,
    coef,
    xs,
    send,
    recv,
    rest_f,
    rest_send,
    rest_recv,
    whole,
    acc,
    stage,
    weights,
    rank,
    base,
    packed_acc,
    packed,
    got,
    cells_s,
    cells_g,
    targets,
    lifted,
    fields,
    edge_s,
    edge_r,
    small_sem,
    in_sem,
    table_sem,
    z_send,
    z_recv,
    send_sem,
    recv_sem,
    rest_ssem,
    rest_rsem,
    route_ssem,
    route_rsem,
    halo_ssem,
    halo_rsem,
):
    me = lax.axis_index("comp")
    tile = lax.axis_index("tile")
    devices = n * n_tile
    number = me * n_tile + tile
    own, rows, width = x_hbm.shape
    cols = width // n
    full = n * own
    main = own // PACK * PACK
    rest = own - main
    groups = main // PACK + (1 if rest else 0)
    steps = rows // PAIR
    halves = rows // PACK
    nb = -(-slots // LANES)
    cells_r, cells_c = result.shape[1], result.shape[2]
    is_top, is_bottom = tile == 0, tile == n_tile - 1
    is_left, is_right = me == 0, me == n - 1
    mesh_id = pl.DeviceIdType.MESH
    above = {"tile": lax.rem(tile + n_tile - 1, n_tile)}
    below = {"tile": lax.rem(tile + 1, n_tile)}
    west_of = {"comp": lax.rem(me + n - 1, n)}
    east_of = {"comp": lax.rem(me + 1, n)}

    def others(act):
        @pl.loop(0, n)
        def _(c):
            comp = lax.rem(me + c, n)
            for t in range(n_tile):
                if t:
                    act(comp, lax.rem(tile + t, n_tile))
                else:
                    pl.when(c > 0)(functools.partial(act, comp, tile))

    smalls = [
        (cx_hbm, cx),
        (cy_hbm, cy),
        (bin_hbm, bins),
        (stress_hbm, stress),
        (orbital_hbm, orbital),
        (grow_hbm, growth),
        (damp_hbm, dissipation),
        (wind_hbm, wind),
        (wet_hbm, wet),
        (owner_hbm, owner),
        (cell_hbm, cell),
        (current_hbm, current),
        (sediment_hbm, sediment),
        (metals_hbm, metals),
        (bed_hbm, bed),
        (roms_hbm, roms),
        (props_hbm, props),
    ]

    def small(i):
        return pltpu.make_async_copy(smalls[i][0], smalls[i][1], small_sem.at[i])

    cuts = [main // PACK * i // PARTS for i in range(PARTS + 1)]
    ends = [c * PACK for c in cuts[:-1]] + [own]
    parts = [(ends[p], ends[p + 1] - ends[p]) for p in range(PARTS)]

    def load(h, p, d):
        first, size = parts[p]
        return pltpu.make_async_copy(
            x_hbm.at[pl.ds(first, size), pl.ds(h * PACK, PACK), pl.ds(d * cols, cols)],
            out.at[pl.ds(d * own + first, size), pl.ds(h * PACK, PACK), :],
            in_sem.at[h, p],
        )

    def loaded(h, p):
        block = out.at[pl.ds(0, n * parts[p][1]), pl.ds(h * PACK, PACK), :]
        return pltpu.make_async_copy(block, block, in_sem.at[h, p])

    def all_of(block, sem):
        return pltpu.make_async_copy(block, block, sem)

    small(0).start()
    small(1).start()
    for p in range(PARTS):
        for d in range(n):
            load(0, p, d).start()

    barrier = pltpu.get_barrier_semaphore()

    def greet(comp, at_tile):
        pl.semaphore_signal(
            barrier, inc=1, device_id={"comp": comp, "tile": at_tile}, device_id_type=mesh_id
        )

    others(greet)
    for h in range(1, halves):
        for p in range(PARTS):
            for d in range(n):
                load(h, p, d).start()
    for i in range(2, len(smalls)):
        small(i).start()
    get_table = pltpu.make_async_copy(transfer_hbm, table.at[pl.ds(0, full)], table_sem.at[0])
    get_table.start()

    def to_columns(values, i):
        for b in range(0, full, LANES):
            size = min(LANES, full - b)
            line = values[pl.ds(b, size)].reshape(1, size)
            columns[i, b : b + size, :] = jnp.broadcast_to(line, (LANES, size)).T

    small(0).wait()
    small(1).wait()
    to_columns(cx, 0)
    to_columns(cy, 1)

    for g in range(groups):
        first = g * PACK if g * PACK < main else own - PACK
        speed_x = columns[0, pl.ds(me * own + first, PACK), :]
        speed_y = columns[1, pl.ds(me * own + first, PACK), :]
        part = slice(g * PACK, (g + 1) * PACK)
        coef[0, part, :] = 1.0 - jnp.abs(speed_x) - jnp.abs(speed_y)
        coef[1, part, :] = jnp.maximum(speed_x, 0.0)
        coef[2, part, :] = -jnp.minimum(speed_x, 0.0)
        coef[3, part, :] = jnp.maximum(speed_y, 0.0)
        coef[4, part, :] = -jnp.minimum(speed_y, 0.0)

    @pl.when(is_top)
    def _():
        xs[0] = jnp.zeros(xs.shape[1:], BF16)
        edge_r[0] = jnp.zeros(edge_r.shape[1:], F32)

    @pl.when(is_bottom)
    def _():
        xs[rows + 1] = jnp.zeros(xs.shape[1:], BF16)
        edge_r[1] = jnp.zeros(edge_r.shape[1:], F32)

    @pl.when(is_left)
    def _():
        edge_r[2] = jnp.zeros(edge_r.shape[1:], F32)

    @pl.when(is_right)
    def _():
        edge_r[3] = jnp.zeros(edge_r.shape[1:], F32)

    def turn_in(c, first_group, last_group, with_rest):
        top = c * QUARTER
        for d in range(n):

            def piece(at, first):
                block = out[pl.ds(d * own + first, PACK), top : top + QUARTER, :].astype(F32)
                xs[1 + top : 1 + top + QUARTER, pl.ds(at, PACK), d * cols : (d + 1) * cols] = (
                    jnp.swapaxes(block, 0, 1).astype(BF16)
                )

            @pl.loop(first_group, last_group)
            def _(g):
                start = pl.multiple_of(g * PACK, PACK)
                piece(start, start)

            if rest and with_rest:
                piece(main, own - PACK)

    def upwind(row, start, is_rest):
        part = pl.ds(start, PACK)
        lane = lax.broadcasted_iota(jnp.int32, (PACK, cols), 1)
        first_lane, last_lane = lane == 0, lane == cols - 1
        kept, from_north, from_south, from_west, from_east = [coef[i, part, :] for i in range(5)]

        def tile_of(at, d):
            return xs[at, part, d * cols : (d + 1) * cols].astype(F32)

        centre = [tile_of(row + 1, d) for d in range(n)]
        right = [pltpu.roll(c, 1, 1) for c in centre]
        left = [pltpu.roll(c, cols - 1, 1) for c in centre]
        nothing = jnp.zeros((PACK, cols), F32)
        for d in range(n):
            west = jnp.where(first_lane, right[d - 1] if d else nothing, right[d])
            east = jnp.where(last_lane, left[d + 1] if d < n - 1 else nothing, left[d])
            moved = (
                kept * centre[d]
                + from_north * tile_of(row, d)
                + from_south * tile_of(row + 2, d)
                + from_west * west
                + from_east * east
            )
            if is_rest:
                rest_f[d, pl.ds(row * rest, rest), :] = moved[PACK - rest :]
            else:
                send[d, row, part, :] = moved.astype(BF16)

    def remote(row, count, first, size, o):
        here = pl.ds(row, count), pl.ds(first, size)
        target = lax.rem(me + o, n)
        return pltpu.make_async_remote_copy(
            src_ref=send.at[target, *here],
            dst_ref=recv.at[me, *here],
            send_sem=send_sem.at[0],
            recv_sem=recv_sem.at[row],
            device_id={"comp": target},
            device_id_type=mesh_id,
        )

    def remote_rest(o, source, target):
        return pltpu.make_async_remote_copy(
            src_ref=rest_send.at[target],
            dst_ref=rest_recv.at[source],
            send_sem=rest_ssem.at[0],
            recv_sem=rest_rsem.at[0],
            device_id={"comp": target},
            device_id_type=mesh_id,
        )

    def sweep(row, count, first_group, last_group):
        size = last_group - first_group

        @pl.loop(0, count * size)
        def _(i):
            start = pl.multiple_of((first_group + lax.rem(i, size)) * PACK, PACK)
            upwind(row + i // size, start, False)

    def scatter(row, count, first, size):
        for o in range(1, n):
            remote(row, count, first, size, o).start()

    def spread_rows(row, count):
        sweep(row, count, 0, main // PACK)
        scatter(row, count, 0, main)
        here = pl.ds(row, count)
        recv[me, here] = send[me, here]

    for p in range(PARTS):
        loaded(0, p).wait()
        turn_in(0, cuts[p], cuts[p + 1], p == PARTS - 1)
        sweep(PAIR, PAIR, cuts[p], cuts[p + 1])
        if p == 0:
            pl.semaphore_wait(barrier, devices - 1)
        scatter(PAIR, PAIR, cuts[p] * PACK, (cuts[p + 1] - cuts[p]) * PACK)
    recv[me, PAIR : 2 * PAIR] = send[me, PAIR : 2 * PAIR]
    spread_rows(2 * PAIR, PAIR)
    for h in range(1, halves):
        for p in range(PARTS):
            loaded(h, p).wait()
    last_quarter = rows // QUARTER - 1
    turn_in(last_quarter, 0, main // PACK, True)

    to_below = pltpu.make_async_remote_copy(
        src_ref=xs.at[pl.ds(rows, 1)],
        dst_ref=xs.at[pl.ds(0, 1)],
        send_sem=z_send.at[0],
        recv_sem=z_recv.at[0],
        device_id=below,
        device_id_type=mesh_id,
    )
    to_above = pltpu.make_async_remote_copy(
        src_ref=xs.at[pl.ds(1, 1)],
        dst_ref=xs.at[pl.ds(rows + 1, 1)],
        send_sem=z_send.at[1],
        recv_sem=z_recv.at[1],
        device_id=above,
        device_id_type=mesh_id,
    )

    @pl.when(jnp.logical_not(is_bottom))
    def _():
        to_below.start()

    @pl.when(jnp.logical_not(is_top))
    def _():
        to_above.start()

    turn_in(1, 0, main // PACK, True)
    spread_rows(3 * PAIR, PAIR)
    for c in range(2, last_quarter):
        turn_in(c, 0, main // PACK, True)

    per_quarter = QUARTER // PAIR

    spread_rows(QUARTER, QUARTER)

    @pl.when(jnp.logical_not(is_top))
    def _():
        to_below.wait_recv()

    @pl.when(jnp.logical_not(is_bottom))
    def _():
        to_above.wait_recv()

    if rest:

        @pl.loop(0, rows)
        def _(i):
            upwind(i, main, True)

    if rest:
        rest_send[...] = rest_f[...].astype(BF16)
        for o in range(1, n):
            remote_rest(o, me, lax.rem(me + o, n)).start()
        rest_recv[me] = rest_send[me]

    spread_rows(0, PAIR)

    for i in range(2, len(smalls)):
        small(i).wait()

    lane_d = lax.broadcasted_iota(jnp.int32, (devices, LANES), 0)
    up_to = lax.broadcasted_iota(jnp.int32, (LANES, 2 * LANES), 0)
    at = lax.broadcasted_iota(jnp.int32, (LANES, 2 * LANES), 1)
    counting = jnp.where(jnp.logical_or(up_to < at, at >= LANES), 1.0, 0.0).astype(BF16)
    base[...] = jnp.zeros(base.shape, F32)

    @pl.loop(0, rows)
    def _(r):
        hit = jnp.where(owner[pl.ds(r, 1), :] == lane_d, 1.0, 0.0)
        counts = jnp.dot(hit.astype(BF16), counting, preferred_element_type=F32)
        before = hit * (counts[:, :LANES] + base[...])
        rank[pl.ds(r, 1), :] = jnp.sum(before, axis=0, keepdims=True).astype(jnp.int32)
        base[...] += counts[:, LANES:]

    sub = lax.broadcasted_iota(jnp.int32, (PACK, LANES), 0)
    slot_lane = lax.broadcasted_iota(jnp.int32, (LANES, LANES), 0)
    owner_of = lax.broadcasted_iota(jnp.int32, (devices, PACK, LANES), 0)

    def pack(row, items):
        place = rank[pl.ds(row, 1), :]
        block, lane = place // LANES, lax.rem(place, LANES)
        rows_of = jnp.zeros((PACK, LANES), F32)
        for f in range(len(items)):
            for b in range(nb):
                here = jnp.logical_and(sub == f * nb + b, block == b)
                rows_of = jnp.where(here, items[f], rows_of)
        mine = owner[pl.ds(row, 1), :][None] == owner_of
        spread = jnp.where(mine, rows_of[None], 0.0).astype(BF16)
        onehot = jnp.where(lane == slot_lane, 1.0, 0.0).astype(BF16)
        return spread.reshape(devices * PACK, LANES), onehot

    def pack_rows(row, items):
        halves_of = [pack(row + a, items[a]) for a in range(len(items))]
        packed_acc[...] += nt_dot(
            jnp.concatenate([h[0] for h in halves_of], axis=1),
            jnp.concatenate([h[1] for h in halves_of], axis=1),
        )

    routes = [(cells_s, cells_g), (packed, got)]

    def send_packed(which):
        source, target = routes[which]
        count = source.shape[1]
        block = packed_acc[...].astype(BF16).reshape(devices, PACK, LANES)
        source[...] = block[:, :count, :]

        def start(comp, at_tile):
            pltpu.make_async_remote_copy(
                src_ref=source.at[comp * n_tile + at_tile],
                dst_ref=target.at[number],
                send_sem=route_ssem.at[which],
                recv_sem=route_rsem.at[which],
                device_id={"comp": comp, "tile": at_tile},
                device_id_type=mesh_id,
            ).start()

        others(start)
        target[number] = source[number]

    def wait_packed(which):
        block = routes[which][1].at[pl.ds(0, devices - 1)]
        all_of(block, route_rsem.at[which]).wait()

    packed_acc[...] = jnp.zeros(packed_acc.shape, F32)

    @pl.loop(0, steps)
    def _(i):
        items = []
        for a in range(PAIR):
            c = cell[pl.ds(i * PAIR + a, 1), :]
            items.append([(c // cells_c).astype(F32), lax.rem(c, cells_c).astype(F32)])
        pack_rows(i * PAIR, items)

    send_packed(0)
    @pl.loop(2, last_quarter)
    def _(c):
        spread_rows(c * QUARTER, QUARTER)

    @pl.loop(per_quarter * last_quarter, steps - 1)
    def _(q):
        spread_rows(q * PAIR, PAIR)

    @pl.loop(rows - PAIR, rows)
    def _(row):
        spread_rows(row, 1)

    to_columns(dissipation, 0)
    to_columns(growth, 1)
    columns[...] = WAVE_STEP * columns[...]

    packed_acc[...] = jnp.zeros(packed_acc.shape, F32)

    get_table.wait()
    bin_high, bin_low = split_two(bins[...].reshape(1, full))
    which = lax.broadcasted_iota(jnp.int32, (PACK, full), 0)
    table[full : full + PACK, :] = jnp.where(
        which == 0, bin_high.astype(F32), jnp.where(which == 1, bin_low.astype(F32), 0.0)
    ).astype(BF16)
    orbit = split_two(orbital[...].reshape(1, full))
    push = split_two(stress[...])
    weight = jnp.zeros((PACK, full), F32)
    for half in range(2):
        lines = [push[half][0:1], push[half][1:2], orbit[half]]
        for f in range(3):
            weight = jnp.where(which == 3 * half + f, lines[f].astype(F32), weight)
    weights[...] = weight.astype(BF16)

    band = 3 * PACK if full % (3 * PACK) == 0 else PACK

    def mix(row, count):
        wide = count * cols
        for s in range(n):
            for a in range(count):
                span = slice(a * cols, (a + 1) * cols)
                whole[s * own : s * own + main, span] = recv[s, row + a].astype(F32)
                if rest:
                    whole[s * own + main : (s + 1) * own, span] = rest_f[
                        s, pl.ds((row + a) * rest, rest), :
                    ]
        acc[:, :wide] = jnp.dot(
            table[...], whole[:, :wide].astype(BF16), preferred_element_type=F32
        )
        total = acc[full : full + 1, :wide] + acc[full + 1 : full + 2, :wide]
        ratio = total / (total + 1.0)
        gust = jnp.concatenate([wind[pl.ds(row + a, 1), :] for a in range(count)], axis=1)
        open_water = jnp.concatenate(
            [wet[pl.ds(row + a, 1), :].astype(F32) for a in range(count)], axis=1
        )
        spot = lax.rem(row, QUARTER)

        @pl.loop(0, full // band)
        def _(b):
            part = pl.ds(pl.multiple_of(b * band, band), band)
            damping, growing = columns[0, part, :], columns[1, part, :]
            for a in range(count):
                span = slice(a * cols, (a + 1) * cols)
                gain = 1.0 - damping * ratio[:, span] + growing * gust[:, span]
                relaxed = WAVE_STEP * acc[part, span] + whole[part, span] * gain
                fresh = open_water[:, span] * jnp.maximum(relaxed, 0.0)
                stage[spot + a, part, :] = fresh.astype(BF16)

        fresh_all = jnp.concatenate([stage[spot + a] for a in range(count)], axis=1)
        pulled = jnp.dot(weights[...], fresh_all, preferred_element_type=F32)
        forces = pulled[0:3] + pulled[3:6]
        pack_rows(
            row,
            [
                [forces[f : f + 1, a * cols : (a + 1) * cols] for f in range(3)]
                for a in range(count)
            ],
        )

    def wait_rows(row, count):
        block = recv.at[pl.ds(0, n - 1), pl.ds(row, count)]
        all_of(block, recv_sem.at[row]).wait()

    def mix_step(q):
        wait_rows(q * PAIR, PAIR)
        mix(q * PAIR, PAIR)

    def turn_out(c):
        @pl.loop(0, full // PACK)
        def _(g):
            part = pl.ds(pl.multiple_of(g * PACK, PACK), PACK)
            block = stage[:, part, :].astype(F32)
            out[part, c * QUARTER : (c + 1) * QUARTER, :] = jnp.swapaxes(block, 0, 1).astype(BF16)

    if rest:
        all_of(rest_recv.at[pl.ds(0, n - 1)], rest_rsem.at[0]).wait()
        rest_f[...] = rest_recv[...].astype(F32)

    @pl.loop(0, per_quarter)
    def _(step):
        mix_step(lax.rem(step + 1, per_quarter))

    turn_out(0)

    for c in range(1, rows // QUARTER):
        if c == last_quarter:
            wait_packed(0)

            @pl.loop(0, devices)
            def _(s):
                cells = cells_g[s].astype(F32)
                for b in range(nb):
                    spot = pl.ds(pl.multiple_of((s * nb + b) * LANES, LANES), LANES)
                    col = cells[nb + b : nb + b + 1, :]
                    targets[:, spot] = jnp.where(col == slot_lane.astype(F32), 1.0, 0.0).astype(BF16)

        if c < last_quarter:

            wait_rows(c * QUARTER, QUARTER)

            @pl.loop(c * per_quarter, (c + 1) * per_quarter)
            def _(q):
                mix(q * PAIR, PAIR)

        else:

            @pl.loop(c * per_quarter, (c + 1) * per_quarter - 1)
            def _(q):
                mix_step(q)

            @pl.loop(rows - PAIR, rows)
            def _(row):
                wait_rows(row, 1)
                mix(row, 1)

        if c == last_quarter:
            send_packed(1)
        turn_out(c)

    classes = sediment.shape[0]
    count = classes + metals.shape[0]
    wetness = roms[...].astype(F32)
    for m in range(count - classes):
        fields[classes + m] = wetness * metals[m]
    wait_packed(1)
    cell_row = lax.broadcasted_iota(jnp.int32, (cells_r, LANES), 0).astype(F32)

    bottom = jnp.zeros((3 * cells_r, cells_c), F32)
    share = min(devices, SHARE)
    for start in range(0, devices, share):

        @pl.loop(0, share)
        def _(i):
            cells = cells_g[start + i].astype(F32)
            force = got[start + i].astype(F32)
            for b in range(nb):
                spot = pl.ds(pl.multiple_of((i * nb + b) * LANES, LANES), LANES)
                hit = cells[b : b + 1, :] == cell_row
                for f in range(3):
                    lifted[f * cells_r : (f + 1) * cells_r, spot] = jnp.where(
                        hit, force[f * nb + b : f * nb + b + 1, :], 0.0
                    ).astype(BF16)

        these = slice(start * nb * LANES, (start + share) * nb * LANES)
        bottom += nt_dot(lifted[...], targets[:, these])

    shear_x = current[0] + bottom[0:cells_r]
    shear_y = current[1] + bottom[cells_r : 2 * cells_r]
    shear = jnp.sqrt(shear_x * shear_x + shear_y * shear_y + bottom[2 * cells_r :])
    low_share = 0.5 / classes
    high_share = 1.0 - (classes - 1) * low_share
    for s in range(classes):
        fraction = jnp.where(bed[...] == s, high_share, low_share)
        rate, critical, settling = [props[i : i + 1, s : s + 1] for i in range(3)]
        erosion = rate * fraction * jnp.maximum(shear / critical - 1.0, 0.0)
        here = sediment[s]
        fields[s] = wetness * (here + SEDIMENT_STEP * (erosion - settling * here))

    held = fields[...]
    def halo(i, device):
        return pltpu.make_async_remote_copy(
            src_ref=edge_s.at[i],
            dst_ref=edge_r.at[i],
            send_sem=halo_ssem.at[i],
            recv_sem=halo_rsem.at[i],
            device_id=device,
            device_id_type=mesh_id,
        )

    halos = [halo(0, below), halo(1, above), halo(2, east_of), halo(3, west_of)]
    sends = [is_bottom, is_top, is_right, is_left]
    receives = [is_top, is_bottom, is_left, is_right]
    edge_s[0] = held[:, cells_r - 1, :]
    edge_s[1] = held[:, 0, :]
    for i in range(2):
        pl.when(jnp.logical_not(sends[i]))(halos[i].start)
    turned = held.reshape(count * cells_r, cells_c).T
    edge_s[2, 0:1, :] = turned[cells_c - 1 :]
    edge_s[3, 0:1, :] = turned[0:1]
    for i in range(2, 4):
        pl.when(jnp.logical_not(sends[i]))(halos[i].start)
    for i in range(4):
        pl.when(jnp.logical_not(receives[i]))(halos[i].wait_recv)

    north = jnp.concatenate([edge_r[0][:, None, :], held[:, :-1, :]], axis=1)
    south = jnp.concatenate([held[:, 1:, :], edge_r[1][:, None, :]], axis=1)
    flat = held.reshape(count * cells_r, cells_c)
    lane = lax.broadcasted_iota(jnp.int32, flat.shape, 1)

    def column(i):
        return jnp.broadcast_to(edge_r[i, 0:1, :], (cells_c, count * cells_r)).T

    west = jnp.where(lane == 0, column(2), pltpu.roll(flat, 1, 1)).reshape(held.shape)
    east = jnp.where(lane == cells_c - 1, column(3), pltpu.roll(flat, cells_c - 1, 1)).reshape(
        held.shape
    )
    beside = north + south + west + east
    result[...] = wetness[None] * (held + DIFFUSION * (beside - 4.0 * held))

    for i in range(4):
        pl.when(jnp.logical_not(sends[i]))(halos[i].wait_send)
    pl.when(jnp.logical_not(is_bottom))(to_below.wait_send)
    pl.when(jnp.logical_not(is_top))(to_above.wait_send)

    all_of(send.at[pl.ds(0, n - 1)], send_sem.at[0]).wait()
    if rest:
        all_of(rest_send.at[pl.ds(0, n - 1)], rest_ssem.at[0]).wait()
    for which in range(2):
        block = routes[which][0].at[pl.ds(0, devices - 1)]
        all_of(block, route_ssem.at[which]).wait()


def finish_kernel(
    fresh,
    diffused,
    partition,
    spectrum_hbm,
    sediment_hbm,
    dissolved_hbm,
    sorbed_hbm,
    dissolved,
    sorbed,
    big_sem,
    field_sem,
):
    full = fresh.shape[0]
    size = -(-full // PIECES)
    spans = [pl.ds(i, min(size, full - i)) for i in range(0, full, size)]
    copies = [
        pltpu.make_async_copy(fresh.at[span], spectrum_hbm.at[span], big_sem.at[i])
        for i, span in enumerate(spans)
    ]
    classes = sediment_hbm.shape[0]
    copies.append(
        pltpu.make_async_copy(diffused.at[pl.ds(0, classes)], sediment_hbm, field_sem.at[0])
    )
    for copy in copies:
        copy.start()
    for m in range(dissolved.shape[0]):
        denominator = 1.0 + sum(
            partition[m : m + 1, s : s + 1] * diffused[s] for s in range(classes)
        )
        spread = diffused[classes + m]
        quotient = spread / denominator
        dissolved[m] = quotient
        sorbed[m] = spread - quotient
    copies.append(pltpu.make_async_copy(dissolved, dissolved_hbm, field_sem.at[1]))
    copies.append(pltpu.make_async_copy(sorbed, sorbed_hbm, field_sem.at[2]))
    for copy in copies[-2:]:
        copy.start()
    for copy in copies:
        copy.wait()


def on_device(
    spectrum,
    courant_x,
    courant_y,
    growth,
    dissipation,
    bin_width,
    transfer,
    stress_weights,
    orbital_weights,
    wind,
    wave_wet,
    owner,
    cell_index,
    current_stress,
    sediment,
    metals,
    bed_class,
    roms_wet,
    class_props,
    partition,
):
    n = lax.axis_size("comp")
    n_tile = lax.axis_size("tile")
    devices = n * n_tile
    own, rows, width = spectrum.shape
    cols = width // n
    full = n * own
    main = own // PACK * PACK
    rest = own - main
    padded = main + (PACK if rest else 0)
    rest_rows = max(rest, 1) * rows
    slots = max(2, 3 * rows * cols // devices)
    nb = -(-slots // LANES)
    steps = rows // PAIR
    classes, cells_r, cells_c = sediment.shape
    count = classes + metals.shape[0]

    operands = (
        spectrum,
        courant_x,
        courant_y,
        growth,
        dissipation,
        bin_width,
        transfer,
        stress_weights,
        orbital_weights,
        wind,
        wave_wet,
        owner.reshape(rows, cols),
        cell_index.reshape(rows, cols),
        current_stress,
        sediment,
        metals,
        bed_class,
        roms_wet,
        class_props,
    )
    vmem = pl.BlockSpec(memory_space=pltpu.VMEM)
    hbm = pl.BlockSpec(memory_space=pltpu.HBM)

    def like(i):
        return pltpu.VMEM(operands[i].shape, operands[i].dtype)

    dma = pltpu.SemaphoreType.DMA
    scratch = [
        *[like(i) for i in range(1, 6)],
        pltpu.VMEM((full + PACK, full), BF16),
        *[like(i) for i in range(7, len(operands))],
        pltpu.VMEM((2, full, LANES), F32),
        pltpu.VMEM((5, padded, cols), F32),
        pltpu.VMEM((rows + 2, padded, width), BF16),
        pltpu.VMEM((n, rows, main, cols), BF16),
        pltpu.VMEM((n, rows, main, cols), BF16),
        pltpu.VMEM((n, rest_rows, cols), F32),
        pltpu.VMEM((n, rest_rows, cols), BF16),
        pltpu.VMEM((n, rest_rows, cols), BF16),
        pltpu.VMEM((full, PAIR * cols), F32),
        pltpu.VMEM((full + PACK, PAIR * cols), F32),
        pltpu.VMEM((QUARTER, full, cols), BF16),
        pltpu.VMEM((PACK, full), BF16),
        pltpu.VMEM((rows, cols), jnp.int32),
        pltpu.VMEM((devices, LANES), F32),
        pltpu.VMEM((devices * PACK, LANES), F32),
        pltpu.VMEM((devices, PACK, LANES), BF16),
        pltpu.VMEM((devices, PACK, LANES), BF16),
        pltpu.VMEM((devices, 2 * nb, LANES), BF16),
        pltpu.VMEM((devices, 2 * nb, LANES), BF16),
        pltpu.VMEM((LANES, devices * nb * LANES), BF16),
        pltpu.VMEM((3 * cells_r, min(devices, SHARE) * nb * LANES), BF16),
        pltpu.VMEM((count, cells_r, cells_c), F32),
        pltpu.VMEM((4, count, cells_c), F32),
        pltpu.VMEM((4, count, cells_c), F32),
        dma((len(operands) - 2,)),
        dma((rows // PACK, PARTS)),
        dma((1,)),
        dma((2,)),
        dma((2,)),
        dma((1,)),
        dma((rows,)),
        dma((1,)),
        dma((1,)),
        dma((2,)),
        dma((2,)),
        dma((4,)),
        dma((4,)),
    ]
    fresh, diffused = pl.pallas_call(
        functools.partial(step_kernel, n, n_tile, slots),
        out_shape=(
            pltpu.VMEM((full, rows, cols), BF16),
            pltpu.VMEM((count, cells_r, cells_c), F32),
        ),
        in_specs=[hbm] * len(operands),
        out_specs=(vmem, vmem),
        scratch_shapes=scratch,
        compiler_params=pltpu.CompilerParams(
            collective_id=0, has_side_effects=True, vmem_limit_bytes=54000 * 1024
        ),
    )(*operands)

    field = jax.ShapeDtypeStruct((classes, cells_r, cells_c), F32)
    metal = jax.ShapeDtypeStruct((count - classes, cells_r, cells_c), F32)
    return tuple(
        pl.pallas_call(
            finish_kernel,
            out_shape=(jax.ShapeDtypeStruct(fresh.shape, fresh.dtype), field, metal, metal),
            in_specs=[pl.BlockSpec(memory_space=pl.ANY), vmem, vmem],
            out_specs=(hbm,) * 4,
            scratch_shapes=[
                pltpu.VMEM(metal.shape, F32),
                pltpu.VMEM(metal.shape, F32),
                dma((PIECES,)),
                dma((3,)),
            ],
            compiler_params=pltpu.CompilerParams(vmem_limit_bytes=4 << 20),
        )(
            pltpu.with_memory_space_constraint(fresh, pltpu.VMEM),
            pltpu.with_memory_space_constraint(diffused, pltpu.VMEM),
            partition,
        )
    )


def solution(mesh):
    replicated = P()
    grid = P("tile", "comp")
    fields = P(None, "tile", "comp")
    in_specs = (
        P("comp", "tile", None),
        *[replicated] * 8,
        grid,
        grid,
        P("tile", "comp", None, None, None),
        P("tile", "comp", None, None),
        fields,
        fields,
        fields,
        grid,
        grid,
        replicated,
        replicated,
    )
    return jax.shard_map(
        on_device, mesh=mesh, in_specs=in_specs, out_specs=(fields,) * 4, check_vma=False
    )
```
